256 devices in a mesh: row: 8 (over y, core), col: 32 (over z, x).
Axes of the slice: x: 4, y: 4, z: 8, core: 2. Of those that a mesh axis runs over, the one named last changes fastest.
Arguments:
- left_values: bfloat16 [16384, 4096], P('col', 'row'), may hold values from 0.1 to 18, as said below
- left_pattern: int32 [128, 32], replicated, may hold values from 0 to 1, as said below
- right_values: bfloat16 [4096, 8192], P('col', 'row'), may hold values from 0.099609375 to 1
- right_pattern: int32 [32, 64], replicated, may hold values from 0 to 1, as said below
Outputs:
- flow: float32 [16384, 8192], P('col', 'row')
The draws below stay inside these ranges and needn't reach their ends.
Inputs may be any that keep to these rules, and one draw needn't show every extreme that they name: left_pattern[i, i % 32] is 1 for every block row i; in every block row, each aligned group of 4 block columns holds at most 2 ones, and some group holds exactly 2. right_pattern[j % 32, j] is 1 for every block column j; in every block row, each aligned group of 8 block columns holds at most 4 ones, and some group holds exactly 4. `left_values`: positive entries.
All inputs are finite; a program needn't handle non-finite values.
Results may differ from the reference program's by a relative error of at most 0.0003.
Values may be sent and summed in bfloat16 or wider, within the bound.
No kernel may reach another device: no remote copies, remote signals or barrier semaphores. Data moves between devices by JAX's collectives and lax.ppermute only.
A program may use at most 64 MiB of HBM per device.

```python
import math
import jax
import jax.numpy as jnp

COL_BLOCKS = 8
SLOTS = 4
BLOCK_ROWS = 128
BLOCK_INNER = 32
BLOCK_COLS = 64
LEFT_GROUP = 4
LEFT_SLOTS = 2
ROWS = 16384
INNER = 4096
COLUMNS = 8192


def draw_left_values(key, part):
    first_key, second_key = jax.random.split(key)
    position = jnp.arange(ROWS, dtype=jnp.float32) / ROWS
    ramp_factor = jnp.power(3.0, 0.5 * position)[:, None]
    base_values = jax.random.uniform(first_key, (ROWS, INNER), jnp.float32, 0.1, 1.0)
    row_scale = jnp.exp(jax.random.uniform(second_key, (ROWS, 1), jnp.float32, 0.0, 0.5 * math.log(10.0)))
    return (base_values * ramp_factor * row_scale).astype(jnp.bfloat16)


def draw_left_pattern(key, part):
    count_key, row_key, group_key, score_key = jax.random.split(key, 4)
    groups = BLOCK_INNER // LEFT_GROUP
    counts = jax.random.randint(count_key, (BLOCK_ROWS, groups), 1, LEFT_SLOTS + 1)
    full_row = jax.random.randint(row_key, (), 0, BLOCK_ROWS)
    full_group = jax.random.randint(group_key, (), 0, groups)
    chosen = (jnp.arange(BLOCK_ROWS)[:, None] == full_row) & (jnp.arange(groups)[None, :] == full_group)
    counts = jnp.where(chosen, LEFT_SLOTS, counts)
    columns = jnp.arange(BLOCK_INNER)
    forced = columns[None, :] == (jnp.arange(BLOCK_ROWS) % BLOCK_INNER)[:, None]
    raw_scores = jax.random.randint(score_key, (BLOCK_ROWS, BLOCK_INNER), 0, 65536)
    scores = raw_scores * BLOCK_INNER + columns[None, :] + forced.astype(jnp.int32) * 33554432
    grouped = scores.reshape(BLOCK_ROWS, groups, LEFT_GROUP)
    ranking = jnp.sum((grouped[:, :, None, :] > grouped[:, :, :, None]).astype(jnp.int32), axis=3)
    chosen_mask = ranking < counts[:, :, None]
    return chosen_mask.reshape(BLOCK_ROWS, BLOCK_INNER).astype(jnp.int32)


def draw_right_pattern(key, part):
    count_key, row_key, group_key, score_key = jax.random.split(key, 4)
    groups = BLOCK_COLS // COL_BLOCKS
    counts = jax.random.randint(count_key, (BLOCK_INNER, groups), 1, SLOTS + 1)
    full_row = jax.random.randint(row_key, (), 0, BLOCK_INNER)
    full_group = jax.random.randint(group_key, (), 0, groups)
    chosen = (jnp.arange(BLOCK_INNER)[:, None] == full_row) & (jnp.arange(groups)[None, :] == full_group)
    counts = jnp.where(chosen, SLOTS, counts)
    columns = jnp.arange(BLOCK_COLS)
    forced = columns[None, :] % BLOCK_INNER == jnp.arange(BLOCK_INNER)[:, None]
    raw_scores = jax.random.randint(score_key, (BLOCK_INNER, BLOCK_COLS), 0, 65536)
    scores = raw_scores * BLOCK_COLS + columns[None, :] + forced.astype(jnp.int32) * 33554432
    grouped = scores.reshape(BLOCK_INNER, groups, COL_BLOCKS)
    ranking = jnp.sum((grouped[:, :, None, :] > grouped[:, :, :, None]).astype(jnp.int32), axis=3)
    chosen_mask = ranking < counts[:, :, None]
    return chosen_mask.reshape(BLOCK_INNER, BLOCK_COLS).astype(jnp.int32)


def block_levels(rng, extent, cuts, smallest, top_value):
    def one(dim, blocks):
        heights = jax.random.uniform(jax.random.fold_in(jax.random.fold_in(rng, 6), dim), (blocks,), jnp.float32, smallest / len(cuts), top_value / len(cuts))
        return jnp.repeat(jnp.exp(heights), extent[dim] // blocks).reshape((-1,) + (1,) * (len(extent) - dim - 1))

    level = one(*cuts[0])
    for cut in cuts[1:]:
        level = level * one(*cut)
    return level


def setup_inputs(seed: int = 0) -> dict:
    keys = jax.random.split(jax.random.key(seed), 5)
    left_values = draw_left_values(jax.random.fold_in(keys[4], 71), 0)
    left_pattern = draw_left_pattern(jax.random.fold_in(keys[4], 71), 0)
    right_values = jnp.clip(0.099609375 + 0.9003906 * jax.random.uniform(keys[2], (INNER, COLUMNS), jnp.float32) ** block_levels(keys[2], (INNER, COLUMNS), ((0, 32), (1, 8)), -0.2, 0.2), 0.099609375, 1.0).astype(jnp.bfloat16)
    right_pattern = draw_right_pattern(jax.random.fold_in(keys[4], 71), 0)
    return dict(left_values=left_values, left_pattern=left_pattern, right_values=right_values, right_pattern=right_pattern)


def expand(values, pattern):
    block_rows, block_cols = pattern.shape
    height, width = values.shape
    shaped = values.reshape(block_rows, height // block_rows, block_cols, width // block_cols)
    masked = shaped * pattern.astype(values.dtype)[:, None, :, None]
    return masked.reshape(height, width)


def reference(left_values, left_pattern, right_values, right_pattern):
    left = expand(left_values, left_pattern).astype(jnp.float32)
    right = expand(right_values, right_pattern).astype(jnp.float32)
    product = jnp.dot(left, right, preferred_element_type=jnp.float32)
    inflated = product * product
    column_mean = jnp.sum(inflated, axis=0) / ROWS
    return inflated / column_mean[None, :]
```

```python
import functools

import jax
import jax.numpy as jnp
from jax import lax
from jax.experimental import pallas as pl
from jax.experimental.pallas import tpu as pltpu
from jax.sharding import Mesh
from jax.sharding import PartitionSpec as P

BLOCK = 128
SLOTS = 4
LEFT_SLOTS = 2
X_SHIFTS = (0, 3, 1, 2)
VMEM_LIMIT = 40 * 1024 * 1024


def lanes(start, blocks=1):
    return pl.ds(pl.multiple_of(start * BLOCK, BLOCK), blocks * BLOCK)


def pack_kernel(right_pattern, left_pattern, right, left, right_out, left_out):
    row = lax.axis_index("row")
    col = lax.axis_index("z") * lax.axis_size("x") + lax.axis_index("x")
    col_blocks = right.shape[1] // BLOCK
    right_out[...] = jnp.zeros_like(right_out)
    slot = jnp.int32(0)
    for j in range(col_blocks):
        present = right_pattern[col, row * col_blocks + j]

        @pl.when(present != 0)
        def _(j=j, slot=slot):
            right_out[:, lanes(slot)] = right[:, j * BLOCK : (j + 1) * BLOCK]

        slot = slot + present
    left_out[...] = jnp.zeros_like(left_out)
    block_rows, inner_blocks = left.shape[0] // BLOCK, left.shape[1] // BLOCK
    for i in range(block_rows):
        rows = slice(i * BLOCK, (i + 1) * BLOCK)
        slot = jnp.int32(0)
        for k in range(inner_blocks):
            present = left_pattern[row * inner_blocks + k, col * block_rows + i]

            @pl.when(present != 0)
            def _(k=k, slot=slot, rows=rows):
                left_out[rows, lanes(slot)] = left[rows, k * BLOCK : (k + 1) * BLOCK]

            slot = slot + present


def pack(right_pattern, left_pattern, right, left):
    return pl.pallas_call(
        pack_kernel,
        out_shape=(
            jax.ShapeDtypeStruct((right.shape[0], SLOTS * BLOCK), right.dtype),
            jax.ShapeDtypeStruct((left.shape[0], LEFT_SLOTS * BLOCK), left.dtype),
        ),
        in_specs=[pl.BlockSpec(memory_space=pltpu.SMEM)] * 2
        + [pl.BlockSpec(memory_space=pltpu.VMEM)] * 2,
        out_specs=[pl.BlockSpec(memory_space=pltpu.VMEM)] * 2,
        compiler_params=pltpu.CompilerParams(vmem_limit_bytes=8 * 1024 * 1024),
        name="pack",
    )(right_pattern, left_pattern, right, left)


def product_kernel(shifts, first, last, right_pattern, left_pattern, *refs):
    refs = list(refs)
    left = refs.pop(0)
    pieces = [refs.pop(0) for _ in range(2 * len(shifts))]
    total = None if first else refs.pop(0)
    out = refs.pop(0)
    sums = refs.pop(0) if last else None
    packed_left, dense_left, dense_right, sem = refs
    row, z, x = lax.axis_index("row"), lax.axis_index("z"), lax.axis_index("x")
    z_size, x_size = lax.axis_size("z"), lax.axis_size("x")
    block_rows = dense_left.shape[0] // BLOCK
    col_blocks = dense_right.shape[1] // BLOCK
    col = z * x_size + x
    groups = [lax.rem(z + shift + z_size, z_size) for shift in shifts]
    copies = [
        pltpu.make_async_copy(left.at[group], packed_left.at[n], sem.at[n])
        for n, group in enumerate(groups)
    ]
    for copy in copies:
        copy.start()
    zero = jnp.zeros((BLOCK, BLOCK), dense_right.dtype)
    for n, group in enumerate(groups):
        for m, x_shift in enumerate(X_SHIFTS):
            k = group * x_size + lax.rem(x + x_shift, x_size)
            piece = pieces[2 * n + m // 2]
            piece_rows = slice((m % 2) * BLOCK, (m % 2 + 1) * BLOCK)
            rows = slice((n * x_size + m) * BLOCK, (n * x_size + m + 1) * BLOCK)
            slot = jnp.int32(0)
            for j in range(col_blocks):
                present = right_pattern[k, row * col_blocks + j]

                @pl.when(present != 0)
                def _(j=j, slot=slot, rows=rows, piece=piece, piece_rows=piece_rows):
                    dense_right[rows, j * BLOCK : (j + 1) * BLOCK] = piece[piece_rows, lanes(slot)]

                @pl.when(present == 0)
                def _(j=j, rows=rows):
                    dense_right[rows, j * BLOCK : (j + 1) * BLOCK] = zero

                slot = slot + present
    for copy in copies:
        copy.wait()
    for n, group in enumerate(groups):
        for i in range(block_rows):
            rows = slice(i * BLOCK, (i + 1) * BLOCK)
            for m, x_shift in enumerate(X_SHIFTS):
                inside = lax.rem(x + x_shift, x_size)
                k = group * x_size + inside
                present = left_pattern[k, col * block_rows + i]
                before = jnp.int32(0)
                for other in range(x_size):
                    there = left_pattern[group * x_size + other, col * block_rows + i]
                    before = before + jnp.where(other < inside, there, 0)
                columns = slice((n * x_size + m) * BLOCK, (n * x_size + m + 1) * BLOCK)

                @pl.when(present != 0)
                def _(n=n, rows=rows, columns=columns, before=before):
                    dense_left[rows, columns] = packed_left[n, rows, lanes(before)]

                @pl.when(present == 0)
                def _(rows=rows, columns=columns):
                    dense_left[rows, columns] = zero

    width = 256

    @pl.loop(0, out.shape[1] // width)
    def _(t):
        columns = pl.ds(pl.multiple_of(t * width, width), width)
        value = jnp.dot(
            dense_left[...], dense_right[:, columns], preferred_element_type=jnp.float32
        )
        if not first:
            value = value + total[:, columns]
        if last:
            value = value * value
            sums[:, columns] = jnp.sum(value, axis=0, keepdims=True)
        out[:, columns] = value


def product(shifts, right_pattern, left_pattern, left, pieces, total, last):
    rows, cols = left.shape[1], right_pattern.shape[1] // 8 * BLOCK
    inner = len(shifts) * 4 * BLOCK
    out_shape = [jax.ShapeDtypeStruct((rows, cols), jnp.float32)]
    if last:
        out_shape.append(jax.ShapeDtypeStruct((1, cols), jnp.float32))
    vmem = pl.BlockSpec(memory_space=pltpu.VMEM)
    operands = [right_pattern, left_pattern, left, *pieces]
    aliases = {}
    if total is not None:
        aliases = {len(operands): 0}
        operands.append(total)
    return pl.pallas_call(
        functools.partial(product_kernel, shifts, total is None, last),
        out_shape=out_shape,
        in_specs=[pl.BlockSpec(memory_space=pltpu.SMEM)] * 2
        + [pl.BlockSpec(memory_space=pl.ANY)]
        + [vmem] * (len(operands) - 3),
        out_specs=[vmem] * len(out_shape),
        scratch_shapes=[
            pltpu.VMEM((len(shifts), rows, LEFT_SLOTS * BLOCK), jnp.bfloat16),
            pltpu.VMEM((rows, inner), jnp.bfloat16),
            pltpu.VMEM((inner, cols), jnp.bfloat16),
            pltpu.SemaphoreType.DMA((len(shifts),)),
        ],
        input_output_aliases=aliases,
        compiler_params=pltpu.CompilerParams(vmem_limit_bytes=VMEM_LIMIT),
        cost_estimate=pl.CostEstimate(
            flops=2 * rows * inner * cols, bytes_accessed=4 * 1024 * 1024, transcendentals=0
        ),
        name="product_" + "_".join(str(s % 8) for s in shifts),
    )(*operands)


def moved(value, axis, step):
    size = lax.axis_size(axis)
    return lax.ppermute(value, axis, [(i, (i + step) % size) for i in range(size)])


def shards(left_values, left_pattern, right_values, right_pattern):
    left_pattern = left_pattern.T
    packed_right, packed_left = pack(right_pattern, left_pattern, right_values, left_values)
    left = lax.all_gather(packed_left, "row", axis=0, tiled=False)
    near = [packed_right] + [moved(packed_right, "x", -shift) for shift in X_SHIFTS[1:]]
    own = [jnp.concatenate(near[:2], 0), jnp.concatenate(near[2:], 0)]
    up, down = own, own
    blocks = {0: own}
    for step in range(1, 5):
        up = [moved(piece, "z", 1) for piece in up]
        blocks[-step] = up
        if step < 4:
            down = [moved(piece, "z", -1) for piece in down]
            blocks[step] = down
    total = None
    for shifts in ((0, -1, 1), (-2, 2), (-3, 3), (-4,)):
        pieces = [piece for shift in shifts for piece in blocks[shift]]
        last = shifts == (-4,)
        results = product(shifts, right_pattern, left_pattern, left, pieces, total, last)
        total = results[0]
    sums = results[1]
    count = lax.axis_size("z") * lax.axis_size("x")
    spread = lax.all_to_all(
        jnp.broadcast_to(sums, (count, sums.shape[1])), ("z", "x"), 0, 0, tiled=True
    )
    column_mean = jnp.sum(spread, axis=0) / (total.shape[0] * count)
    return total / column_mean[None, :]


def solution(mesh):
    finer = Mesh(mesh.devices.reshape(mesh.shape["row"], 8, 4), ("row", "z", "x"))
    return jax.shard_map(
        shards,
        mesh=finer,
        in_specs=(P(("z", "x"), "row"), P(), P(("z", "x"), "row"), P()),
        out_specs=P(("z", "x"), "row"),
        check_vma=False,
    )
```

```python
import functools

import jax
import jax.numpy as jnp
from jax import lax
from jax.experimental import pallas as pl
from jax.experimental.pallas import tpu as pltpu
from jax.sharding import Mesh
from jax.sharding import PartitionSpec as P

BLOCK = 128
SLOTS = 4
LEFT_SLOTS = 2
X_SHIFTS = (0, 3, 1, 2)
VMEM_LIMIT = 20 * 1024 * 1024


def lanes(start, blocks=1):
    return pl.ds(pl.multiple_of(start * BLOCK, BLOCK), blocks * BLOCK)


def pack_kernel(right_pattern, left_pattern, right, left, right_out, left_out, sem):
    row = lax.axis_index("row")
    col = lax.axis_index("z") * lax.axis_size("x") + lax.axis_index("x")
    col_blocks = right.shape[1] // BLOCK
    copies = []
    slot = jnp.int32(0)
    for j in range(col_blocks):
        present = right_pattern[col, row * col_blocks + j]
        copies.append((
            present,
            pltpu.make_async_copy(
                right.at[:, j * BLOCK : (j + 1) * BLOCK],
                right_out.at[:, lanes(jnp.minimum(slot, SLOTS - 1))],
                sem.at[len(copies)],
            ),
        ))
        slot = slot + present
    block_rows, inner_blocks = left.shape[0] // BLOCK, left.shape[1] // BLOCK
    for i in range(block_rows):
        rows = slice(i * BLOCK, (i + 1) * BLOCK)
        slot = jnp.int32(0)
        for k in range(inner_blocks):
            present = left_pattern[row * inner_blocks + k, col * block_rows + i]
            copies.append((
                present,
                pltpu.make_async_copy(
                    left.at[rows, k * BLOCK : (k + 1) * BLOCK],
                    left_out.at[rows, lanes(jnp.minimum(slot, LEFT_SLOTS - 1))],
                    sem.at[len(copies)],
                ),
            ))
            slot = slot + present
    for present, copy in copies:
        pl.when(present != 0)(copy.start)
    for present, copy in copies:
        pl.when(present != 0)(copy.wait)


def pack(right_pattern, left_pattern, right, left):
    count = right.shape[1] // BLOCK + left.shape[0] // BLOCK * (left.shape[1] // BLOCK)
    return pl.pallas_call(
        pack_kernel,
        out_shape=(
            jax.ShapeDtypeStruct((right.shape[0], SLOTS * BLOCK), right.dtype),
            jax.ShapeDtypeStruct((left.shape[0], LEFT_SLOTS * BLOCK), left.dtype),
        ),
        in_specs=[pl.BlockSpec(memory_space=pltpu.SMEM)] * 2
        + [pl.BlockSpec(memory_space=pl.ANY)] * 2,
        out_specs=[pl.BlockSpec(memory_space=pl.ANY)] * 2,
        scratch_shapes=[pltpu.SemaphoreType.DMA((count,))],
        name="pack",
    )(right_pattern, left_pattern, right, left)


def product_kernel(shifts, first, last, right_pattern, left_pattern, *refs):
    refs = list(refs)
    left = refs.pop(0)
    pieces = [refs.pop(0) for _ in range(2 * len(shifts))]
    total = None if first else refs.pop(0)
    out = refs.pop(0)
    sums = refs.pop(0) if last else None
    packed_left, packed_right, dense_left, dense_right, sem = refs
    row, z, x = lax.axis_index("row"), lax.axis_index("z"), lax.axis_index("x")
    z_size, x_size = lax.axis_size("z"), lax.axis_size("x")
    block_rows = dense_left.shape[0] // BLOCK
    col_blocks = dense_right.shape[1] // BLOCK
    col = z * x_size + x
    groups = [lax.rem(z + shift + z_size, z_size) for shift in shifts]
    half = pieces[0].shape[0]
    copies = []
    for n, group in enumerate(groups):
        copies.append(pltpu.make_async_copy(left.at[group], packed_left.at[n], sem.at[len(copies)]))
        for h in range(2):
            copies.append(
                pltpu.make_async_copy(
                    pieces[2 * n + h],
                    packed_right.at[pl.ds((2 * n + h) * half, half)],
                    sem.at[len(copies)],
                )
            )
    for copy in copies:
        copy.start()
    left_plan, right_plan = [], []
    for n, group in enumerate(groups):
        for m, x_shift in enumerate(X_SHIFTS):
            inside = lax.rem(x + x_shift, x_size)
            k = group * x_size + inside
            at = slice((n * x_size + m) * BLOCK, (n * x_size + m + 1) * BLOCK)
            slot = jnp.int32(0)
            for j in range(col_blocks):
                present = right_pattern[k, row * col_blocks + j]
                right_plan.append((at, j, present, jnp.minimum(slot, SLOTS - 1)))
                slot = slot + present
            for i in range(block_rows):
                present = left_pattern[k, col * block_rows + i]
                before = jnp.int32(0)
                for other in range(x_size):
                    there = left_pattern[group * x_size + other, col * block_rows + i]
                    before = before + jnp.where(other < inside, there, 0)
                left_plan.append((n, i, at, present, jnp.minimum(before, LEFT_SLOTS - 1)))
    for copy in copies:
        copy.wait()
    zero = jnp.zeros((BLOCK, BLOCK), dense_right.dtype)
    for at, j, present, slot in right_plan:
        value = packed_right[at, lanes(slot)]
        dense_right[at, j * BLOCK : (j + 1) * BLOCK] = jnp.where(present != 0, value, zero)
    for n, i, at, present, slot in left_plan:
        rows = slice(i * BLOCK, (i + 1) * BLOCK)
        value = packed_left[n, rows, lanes(slot)]
        dense_left[rows, at] = jnp.where(present != 0, value, zero)

    width = 256

    @pl.loop(0, out.shape[1] // width)
    def _(t):
        columns = pl.ds(pl.multiple_of(t * width, width), width)
        value = jnp.dot(
            dense_left[...], dense_right[:, columns], preferred_element_type=jnp.float32
        )
        if not first:
            value = value + total[:, columns]
        if last:
            value = value * value
            sums[:, columns] = jnp.sum(value, axis=0, keepdims=True)
        out[:, columns] = value


def product(shifts, right_pattern, left_pattern, left, pieces, total, last):
    rows, cols = left.shape[1], right_pattern.shape[1] // 8 * BLOCK
    inner = len(shifts) * 4 * BLOCK
    out_shape = [jax.ShapeDtypeStruct((rows, cols), jnp.float32)]
    if last:
        out_shape.append(jax.ShapeDtypeStruct((1, cols), jnp.float32))
    vmem = pl.BlockSpec(memory_space=pltpu.VMEM)
    left = pltpu.with_memory_space_constraint(left, pltpu.HBM)
    if not last:
        pieces = [pltpu.with_memory_space_constraint(piece, pltpu.HBM) for piece in pieces]
    operands = [right_pattern, left_pattern, left, *pieces]
    in_specs = [pl.BlockSpec(memory_space=pltpu.SMEM)] * 2
    in_specs += [pl.BlockSpec(memory_space=pl.ANY)] * (len(operands) - 2)
    aliases = {}
    if total is not None:
        aliases = {len(operands): 0}
        operands.append(total)
        in_specs.append(vmem)
    return pl.pallas_call(
        functools.partial(product_kernel, shifts, total is None, last),
        out_shape=out_shape,
        in_specs=in_specs,
        out_specs=[vmem] * len(out_shape),
        scratch_shapes=[
            pltpu.VMEM((len(shifts), rows, LEFT_SLOTS * BLOCK), jnp.bfloat16),
            pltpu.VMEM((inner, SLOTS * BLOCK), jnp.bfloat16),
            pltpu.VMEM((rows, inner), jnp.bfloat16),
            pltpu.VMEM((inner, cols), jnp.bfloat16),
            pltpu.SemaphoreType.DMA((3 * len(shifts),)),
        ],
        input_output_aliases=aliases,
        compiler_params=pltpu.CompilerParams(vmem_limit_bytes=VMEM_LIMIT),
        cost_estimate=pl.CostEstimate(
            flops=2 * rows * inner * cols, bytes_accessed=4 * 1024 * 1024, transcendentals=0
        ),
        name="product_" + "_".join(str(s % 8) for s in shifts),
    )(*operands)


def moved(value, axis, step):
    size = lax.axis_size(axis)
    return lax.ppermute(value, axis, [(i, (i + step) % size) for i in range(size)])


def shards(left_values, left_pattern, right_values, right_pattern):
    left_pattern = left_pattern.T
    packed_right, packed_left = pack(right_pattern, left_pattern, right_values, left_values)
    left = lax.all_gather(packed_left, "row", axis=0, tiled=False)
    near = [packed_right] + [moved(packed_right, "x", -shift) for shift in X_SHIFTS[1:]]
    own = [jnp.concatenate(near[:2], 0), jnp.concatenate(near[2:], 0)]
    up, down = own, own
    blocks = {0: own}
    for step in range(1, 4):
        up = [moved(piece, "z", 1) for piece in up]
        down = [moved(piece, "z", -1) for piece in down]
        if step == 3:
            left, up, down = lax.optimization_barrier((left, up, down))
        blocks[-step], blocks[step] = up, down
    blocks[4] = [moved(up[0], "z", 1), moved(down[1], "z", -1)]
    total = None
    for shifts in ((0, -1, 1, -2, 2), (-3, 3), (4,)):
        pieces = [piece for shift in shifts for piece in blocks[shift]]
        last = shifts == (4,)
        results = product(shifts, right_pattern, left_pattern, left, pieces, total, last)
        total = results[0]
    sums = results[1]
    count = lax.axis_size("z") * lax.axis_size("x")
    spread = lax.all_to_all(
        jnp.broadcast_to(sums, (count, sums.shape[1])), ("z", "x"), 0, 0, tiled=True
    )
    column_mean = jnp.sum(spread, axis=0) / (total.shape[0] * count)
    return total / column_mean[None, :]


def solution(mesh):
    finer = Mesh(mesh.devices.reshape(mesh.shape["row"], 8, 4), ("row", "z", "x"))
    return jax.shard_map(
        shards,
        mesh=finer,
        in_specs=(P(("z", "x"), "row"), P(), P(("z", "x"), "row"), P()),
        out_specs=P(("z", "x"), "row"),
        check_vma=False,
    )
```

```python
import functools

import jax
import jax.numpy as jnp
from jax import lax
from jax.experimental import pallas as pl
from jax.experimental.pallas import tpu as pltpu
from jax.sharding import Mesh
from jax.sharding import PartitionSpec as P

BLOCK = 128
SLOTS = 4
LEFT_SLOTS = 2
SHIFTS = (0, 3, 1, 2)
PLACES = (0, 2, 3, 1)
KERNEL_VMEM = 20 * 1024 * 1024
ROW, COL = ("y", "core"), ("z", "x")


def lanes(start, blocks=1):
    return pl.ds(pl.multiple_of(start * BLOCK, BLOCK), blocks * BLOCK)


def place_of(shift):
    place = jnp.int32(PLACES[3])
    for s in range(3):
        place = jnp.where(shift == s, PLACES[s], place)
    return place


def row_index():
    return lax.axis_index("y") * lax.axis_size("core") + lax.axis_index("core")


def col_index():
    return lax.axis_index("z") * lax.axis_size("x") + lax.axis_index("x")


def pack_right_kernel(pattern, right, out):
    row, col = row_index(), col_index()
    col_blocks = right.shape[1] // BLOCK
    out[...] = jnp.zeros_like(out)
    slot = jnp.int32(0)
    for j in range(col_blocks):
        present = pattern[col, row * col_blocks + j]

        @pl.when(present != 0)
        def _(j=j, slot=slot):
            out[:, lanes(slot)] = right[:, j * BLOCK : (j + 1) * BLOCK]

        slot = slot + present


def pack_left_kernel(pattern, left, out):
    row, col = row_index(), col_index()
    block_rows, inner_blocks = left.shape[0] // BLOCK, left.shape[1] // BLOCK
    out[...] = jnp.zeros_like(out)
    for i in range(block_rows):
        rows = slice(i * BLOCK, (i + 1) * BLOCK)
        slot = jnp.int32(0)
        for k in range(inner_blocks):
            present = pattern[row * inner_blocks + k, col * block_rows + i]

            @pl.when(present != 0)
            def _(k=k, slot=slot, rows=rows):
                out[rows, lanes(slot)] = left[rows, k * BLOCK : (k + 1) * BLOCK]

            slot = slot + present


def pack(kernel, name, pattern, values, slots):
    return pl.pallas_call(
        kernel,
        out_shape=jax.ShapeDtypeStruct((values.shape[0], slots * BLOCK), values.dtype),
        in_specs=[
            pl.BlockSpec(memory_space=pltpu.SMEM),
            pl.BlockSpec(memory_space=pltpu.VMEM),
        ],
        out_specs=pl.BlockSpec(memory_space=pltpu.VMEM),
        compiler_params=pltpu.CompilerParams(vmem_limit_bytes=4 * 1024 * 1024),
        name=name,
    )(pattern, values)


def product_kernel(shifts, first, last, right_pattern, left_pattern, *refs):
    refs = list(refs)
    mine, other = refs.pop(0), refs.pop(0)
    pieces = [refs.pop(0) for _ in range(2 * len(shifts))]
    total = None if first else refs.pop(0)
    out = refs.pop(0)
    sums = refs.pop(0) if last else None
    packed_left, packed_right, dense_left, dense_right, sem = refs
    row, col = row_index(), col_index()
    y, core = lax.axis_index("y"), lax.axis_index("core")
    z, x = lax.axis_index("z"), lax.axis_index("x")
    y_size, z_size, x_size = lax.axis_size("y"), lax.axis_size("z"), lax.axis_size("x")
    cores = lax.axis_size("core")
    block_rows = dense_left.shape[0] // BLOCK
    col_blocks = dense_right.shape[1] // BLOCK
    groups = [lax.rem(z + shift + z_size, z_size) for shift in shifts]
    half = pieces[0].shape[0]
    waits = []
    for n, group in enumerate(groups):
        there = place_of(lax.rem(lax.div(group, cores) - y + y_size, y_size))
        same = lax.rem(group, cores) == core
        for source, wanted in ((mine, same), (other, jnp.logical_not(same))):
            copy = pltpu.make_async_copy(
                source.at[there], packed_left.at[n, :, : LEFT_SLOTS * BLOCK], sem.at[3 * n]
            )
            pl.when(wanted)(copy.start)
        waits.append(copy)
        for h in range(2):
            copy = pltpu.make_async_copy(
                pieces[2 * n + h],
                packed_right.at[pl.ds((2 * n + h) * half, half), : SLOTS * BLOCK],
                sem.at[3 * n + 1 + h],
            )
            copy.start()
            waits.append(copy)
    packed_left[:, :, LEFT_SLOTS * BLOCK :] = jnp.zeros(
        (len(shifts), packed_left.shape[1], BLOCK), packed_left.dtype
    )
    packed_right[:, SLOTS * BLOCK :] = jnp.zeros(
        (packed_right.shape[0], BLOCK), packed_right.dtype
    )
    right_plan, left_plan = [], []
    for n, group in enumerate(groups):
        for inside in range(x_size):
            k = group * x_size + inside
            start = n * x_size * BLOCK
            to = slice(start + inside * BLOCK, start + (inside + 1) * BLOCK)
            place = place_of(lax.rem(inside - x + x_size, x_size))
            at = pl.ds(pl.multiple_of(start + place * BLOCK, BLOCK), BLOCK)
            slot = jnp.int32(0)
            for j in range(col_blocks):
                present = right_pattern[k, row * col_blocks + j]
                source = jnp.where(present != 0, jnp.minimum(slot, SLOTS), SLOTS)
                right_plan.append((at, to, j, source))
                slot = slot + present
        for i in range(block_rows):
            slot = jnp.int32(0)
            for inside in range(x_size):
                to = lanes(n * x_size + inside)
                present = left_pattern[group * x_size + inside, col * block_rows + i]
                source = jnp.where(present != 0, jnp.minimum(slot, LEFT_SLOTS), LEFT_SLOTS)
                left_plan.append((n, i, inside, source))
                slot = slot + present
    for copy in waits:
        copy.wait()
    for at, to, j, source in right_plan:
        dense_right[to, j * BLOCK : (j + 1) * BLOCK] = packed_right[at, lanes(source)]
    for n, i, inside, source in left_plan:
        rows = slice(i * BLOCK, (i + 1) * BLOCK)
        start = (n * x_size + inside) * BLOCK
        dense_left[rows, start : start + BLOCK] = packed_left[n, rows, lanes(source)]

    width = 256

    @pl.loop(0, out.shape[1] // width)
    def _(t):
        columns = pl.ds(pl.multiple_of(t * width, width), width)
        value = jnp.dot(
            dense_left[...], dense_right[:, columns], preferred_element_type=jnp.float32
        )
        if not first:
            value = value + total[:, columns]
        if last:
            value = value * value
            sums[:, columns] = jnp.sum(value, axis=0, keepdims=True)
        out[:, columns] = value


def product(shifts, right_pattern, left_pattern, left, pieces, total, last):
    rows, cols = left[0].shape[1], right_pattern.shape[1] // 8 * BLOCK
    inner = len(shifts) * 4 * BLOCK
    out_shape = [jax.ShapeDtypeStruct((rows, cols), jnp.float32)]
    if last:
        out_shape.append(jax.ShapeDtypeStruct((1, cols), jnp.float32))
    vmem = pl.BlockSpec(memory_space=pltpu.VMEM)
    left = [pltpu.with_memory_space_constraint(value, pltpu.HBM) for value in left]
    if not last:
        pieces = [pltpu.with_memory_space_constraint(piece, pltpu.HBM) for piece in pieces]
    operands = [right_pattern, left_pattern, *left, *pieces]
    in_specs = [pl.BlockSpec(memory_space=pltpu.SMEM)] * 2
    in_specs += [pl.BlockSpec(memory_space=pl.ANY)] * (len(operands) - 2)
    aliases = {}
    if total is not None:
        aliases = {len(operands): 0}
        operands.append(total)
        in_specs.append(vmem)
    return pl.pallas_call(
        functools.partial(product_kernel, shifts, total is None, last),
        out_shape=out_shape,
        in_specs=in_specs,
        out_specs=[vmem] * len(out_shape),
        scratch_shapes=[
            pltpu.VMEM((len(shifts), rows, (LEFT_SLOTS + 1) * BLOCK), jnp.bfloat16),
            pltpu.VMEM((inner, (SLOTS + 1) * BLOCK), jnp.bfloat16),
            pltpu.VMEM((rows, inner), jnp.bfloat16),
            pltpu.VMEM((inner, cols), jnp.bfloat16),
            pltpu.SemaphoreType.DMA((3 * len(shifts),)),
        ],
        input_output_aliases=aliases,
        compiler_params=pltpu.CompilerParams(vmem_limit_bytes=KERNEL_VMEM),
        cost_estimate=pl.CostEstimate(
            flops=2 * rows * inner * cols, bytes_accessed=4 * 1024 * 1024, transcendentals=0
        ),
        name="product_" + "_".join(str(s % 8) for s in shifts),
    )(*operands)


def moved(value, axis, step):
    size = lax.axis_size(axis)
    return lax.ppermute(value, axis, [(i, (i + step) % size) for i in range(size)])


def shards(left_values, left_pattern, right_values, right_pattern):
    left_pattern = left_pattern.T
    packed_right = pack(pack_right_kernel, "pack_right", right_pattern, right_values, SLOTS)
    near = [packed_right] + [moved(packed_right, "x", -shift) for shift in SHIFTS[1:]]
    packed_left = pack(pack_left_kernel, "pack_left", left_pattern, left_values, LEFT_SLOTS)
    packed_left, near = lax.optimization_barrier((packed_left, near))
    own = [jnp.concatenate(near[:2], 0), jnp.concatenate(near[2:], 0)]
    blocks = {0: own}
    up = [moved(piece, "z", 1) for piece in own]
    down = [moved(piece, "z", -1) for piece in own]
    columns = [packed_left] + [moved(packed_left, "y", -shift) for shift in SHIFTS[1:]]
    columns, up, down = lax.optimization_barrier((columns, up, down))
    mine = jnp.stack(columns)
    blocks[-1], blocks[1] = up, down
    up = [moved(piece, "z", 1) for piece in up]
    down = [moved(piece, "z", -1) for piece in down]
    other = moved(mine, "core", 1)
    left = (mine, other)
    blocks[-2], blocks[2] = up, down
    up = [moved(piece, "z", 1) for piece in up]
    down = [moved(piece, "z", -1) for piece in down]
    left, up, down = lax.optimization_barrier((left, up, down))
    blocks[-3], blocks[3] = up, down
    blocks[4] = [moved(up[0], "z", 1), moved(down[1], "z", -1)]

    def add(shifts, total, last=False):
        pieces = [piece for shift in shifts for piece in blocks[shift]]
        return product(shifts, right_pattern, left_pattern, left, pieces, total, last)

    (total,) = add((0, -1, 1, -2, 2, -3, 3), None)
    total, sums = add((4,), total, True)
    count = lax.axis_size("z") * lax.axis_size("x")
    spread = lax.all_to_all(
        jnp.broadcast_to(sums, (count, sums.shape[1])), COL, 0, 0, tiled=True
    )
    column_mean = jnp.sum(spread, axis=0) / (total.shape[0] * count)
    return total / column_mean[None, :]


def solution(mesh):
    finer = Mesh(mesh.devices.reshape(4, 2, 8, 4), (*ROW, *COL))
    return jax.shard_map(
        shards,
        mesh=finer,
        in_specs=(P(COL, ROW), P(), P(COL, ROW), P()),
        out_specs=P(COL, ROW),
        check_vma=False,
    )
```

```python
import functools

import jax
import jax.numpy as jnp
from jax import lax
from jax.experimental import pallas as pl
from jax.experimental.pallas import tpu as pltpu
from jax.sharding import Mesh
from jax.sharding import PartitionSpec as P

BLOCK = 128
SLOTS = 4
LEFT_SLOTS = 2
SHIFTS = (0, 3, 1, 2)
PLACES = (0, 2, 3, 1)
FAR = (-3, 3, 4)
KERNEL_VMEM = 24 * 1024 * 1024
ROW, COL = ("y", "core"), ("z", "x")


def lanes(start, blocks=1):
    return pl.ds(pl.multiple_of(start * BLOCK, BLOCK), blocks * BLOCK)


def place_of(shift):
    place = jnp.int32(PLACES[3])
    for s in range(3):
        place = jnp.where(shift == s, PLACES[s], place)
    return place


def row_index():
    return lax.axis_index("y") * lax.axis_size("core") + lax.axis_index("core")


def col_index():
    return lax.axis_index("z") * lax.axis_size("x") + lax.axis_index("x")


def pack_right_kernel(pattern, right, out):
    row, col = row_index(), col_index()
    col_blocks = right.shape[1] // BLOCK
    out[...] = jnp.zeros_like(out)
    slot = jnp.int32(0)
    for j in range(col_blocks):
        present = pattern[col, row * col_blocks + j]

        @pl.when(present != 0)
        def _(j=j, slot=slot):
            out[:, lanes(slot)] = right[:, j * BLOCK : (j + 1) * BLOCK]

        slot = slot + present


def pack_left_kernel(pattern, left, out):
    row, col = row_index(), col_index()
    block_rows, inner_blocks = left.shape[0] // BLOCK, left.shape[1] // BLOCK
    out[...] = jnp.zeros_like(out)
    for i in range(block_rows):
        rows = slice(i * BLOCK, (i + 1) * BLOCK)
        slot = jnp.int32(0)
        for k in range(inner_blocks):
            present = pattern[row * inner_blocks + k, col * block_rows + i]

            @pl.when(present != 0)
            def _(k=k, slot=slot, rows=rows):
                out[rows, lanes(slot)] = left[rows, k * BLOCK : (k + 1) * BLOCK]

            slot = slot + present


def pack(kernel, name, pattern, values, slots):
    return pl.pallas_call(
        kernel,
        out_shape=jax.ShapeDtypeStruct((values.shape[0], slots * BLOCK), values.dtype),
        in_specs=[
            pl.BlockSpec(memory_space=pltpu.SMEM),
            pl.BlockSpec(memory_space=pltpu.VMEM),
        ],
        out_specs=pl.BlockSpec(memory_space=pltpu.VMEM),
        compiler_params=pltpu.CompilerParams(vmem_limit_bytes=4 * 1024 * 1024),
        name=name,
    )(pattern, values)


def product_kernel(blocks, copies, first, last, *refs):
    refs = list(refs)
    right_hbm, left_hbm, mine, other = [refs.pop(0) for _ in range(4)]
    pieces = [refs.pop(0) for _ in range(1 + max(copy[0] for copy in copies))]
    total = None if first else refs.pop(0)
    out = refs.pop(0)
    sums = refs.pop(0) if last else None
    right_pattern, left_pattern, plan, *refs = refs
    packed_left, packed_right, dense_left, dense_right, sem, pattern_sem = refs
    row, col = row_index(), col_index()
    y, core = lax.axis_index("y"), lax.axis_index("core")
    z, x = lax.axis_index("z"), lax.axis_index("x")
    y_size, z_size, x_size = lax.axis_size("y"), lax.axis_size("z"), lax.axis_size("x")
    cores = lax.axis_size("core")
    block_rows = dense_left.shape[0] // BLOCK
    col_blocks = dense_right.shape[1] // BLOCK
    z_shifts = sorted({block[0] for block in blocks})
    groups = [lax.rem(z + shift + z_size, z_size) for shift in z_shifts]
    patterns = [
        pltpu.make_async_copy(right_hbm, right_pattern, pattern_sem.at[0]),
        pltpu.make_async_copy(left_hbm, left_pattern, pattern_sem.at[1]),
    ]
    for copy in patterns:
        copy.start()
    waits = []
    for n, group in enumerate(groups):
        there = place_of(lax.rem(lax.div(group, cores) - y + y_size, y_size))
        same = lax.rem(group, cores) == core
        for source, wanted in ((mine, same), (other, jnp.logical_not(same))):
            copy = pltpu.make_async_copy(
                source.at[there], packed_left.at[n, :, : LEFT_SLOTS * BLOCK], sem.at[n]
            )
            pl.when(wanted)(copy.start)
        waits.append(copy)
    for c, (piece, start, rows, to) in enumerate(copies):
        copy = pltpu.make_async_copy(
            pieces[piece].at[pl.ds(start, rows)],
            packed_right.at[pl.ds(to, rows), : SLOTS * BLOCK],
            sem.at[len(groups) + c],
        )
        copy.start()
        waits.append(copy)
    packed_left[:, :, LEFT_SLOTS * BLOCK :] = jnp.zeros(
        (len(groups), packed_left.shape[1], BLOCK), packed_left.dtype
    )
    packed_right[:, SLOTS * BLOCK :] = jnp.zeros(
        (packed_right.shape[0], BLOCK), packed_right.dtype
    )
    for copy in patterns:
        copy.wait()
    for n, group in enumerate(groups):
        for i in range(block_rows):
            slot = jnp.int32(0)
            for inside in range(x_size):
                present = left_pattern[group * x_size + inside, col * block_rows + i]
                source = jnp.where(present != 0, jnp.minimum(slot, LEFT_SLOTS), LEFT_SLOTS)
                plan[(n * block_rows + i) * x_size + inside] = source
                slot = slot + present
    right_plan, left_plan = [], []
    for b, (z_shift, x_shift) in enumerate(blocks):
        n = z_shifts.index(z_shift)
        inside = lax.rem(x + x_shift, x_size)
        k = groups[n] * x_size + inside
        slot = jnp.int32(0)
        for j in range(col_blocks):
            present = right_pattern[k, row * col_blocks + j]
            right_plan.append((b, j, jnp.where(present != 0, jnp.minimum(slot, SLOTS), SLOTS)))
            slot = slot + present
        for i in range(block_rows):
            left_plan.append((n, b, i, plan[(n * block_rows + i) * x_size + inside]))
    for copy in waits:
        copy.wait()
    for b, j, source in right_plan:
        rows = slice(b * BLOCK, (b + 1) * BLOCK)
        dense_right[rows, j * BLOCK : (j + 1) * BLOCK] = packed_right[rows, lanes(source)]
    for n, b, i, source in left_plan:
        rows = slice(i * BLOCK, (i + 1) * BLOCK)
        dense_left[rows, b * BLOCK : (b + 1) * BLOCK] = packed_left[n, rows, lanes(source)]

    width = 256 if last else out.shape[1]

    @pl.loop(0, out.shape[1] // width)
    def _(t):
        columns = pl.ds(pl.multiple_of(t * width, width), width)
        value = jnp.dot(
            dense_left[...], dense_right[:, columns], preferred_element_type=jnp.float32
        )
        if not first:
            value = value + total[:, columns]
        if last:
            value = value * value
            sums[:, columns] = jnp.sum(value, axis=0, keepdims=True)
        out[:, columns] = value


def product(blocks, copies, right_pattern, left_pattern, left, pieces, total, last):
    rows, cols = left[0].shape[1], right_pattern.shape[1] // 8 * BLOCK
    inner = len(blocks) * BLOCK
    groups = len({block[0] for block in blocks})
    out_shape = [jax.ShapeDtypeStruct((rows, cols), jnp.float32)]
    if last:
        out_shape.append(jax.ShapeDtypeStruct((1, cols), jnp.float32))
    vmem = pl.BlockSpec(memory_space=pltpu.VMEM)
    left = [pltpu.with_memory_space_constraint(value, pltpu.HBM) for value in left]
    if not last:
        pieces = [pltpu.with_memory_space_constraint(piece, pltpu.HBM) for piece in pieces]
    operands = [right_pattern, left_pattern, *left, *pieces]
    in_specs = [pl.BlockSpec(memory_space=pl.ANY)] * len(operands)
    aliases = {}
    if total is not None:
        aliases = {len(operands): 0}
        operands.append(total)
        in_specs.append(vmem)
    return pl.pallas_call(
        functools.partial(product_kernel, blocks, copies, total is None, last),
        out_shape=out_shape,
        in_specs=in_specs,
        out_specs=[vmem] * len(out_shape),
        scratch_shapes=[
            pltpu.SMEM(right_pattern.shape, jnp.int32),
            pltpu.SMEM(left_pattern.shape, jnp.int32),
            pltpu.SMEM((groups * rows // BLOCK * 4,), jnp.int32),
            pltpu.VMEM((groups, rows, (LEFT_SLOTS + 1) * BLOCK), jnp.bfloat16),
            pltpu.VMEM((inner, (SLOTS + 1) * BLOCK), jnp.bfloat16),
            pltpu.VMEM((rows, inner), jnp.bfloat16),
            pltpu.VMEM((inner, cols), jnp.bfloat16),
            pltpu.SemaphoreType.DMA((groups + len(copies),)),
            pltpu.SemaphoreType.DMA((2,)),
        ],
        input_output_aliases=aliases,
        compiler_params=pltpu.CompilerParams(vmem_limit_bytes=KERNEL_VMEM),
        cost_estimate=pl.CostEstimate(
            flops=2 * rows * inner * cols, bytes_accessed=4 * 1024 * 1024, transcendentals=0
        ),
        name="product_last" if last else "product_first",
    )(*operands)


def moved(value, axis, step):
    size = lax.axis_size(axis)
    return lax.ppermute(value, axis, [(i, (i + step) % size) for i in range(size)])


def shards(left_values, left_pattern, right_values, right_pattern):
    left_pattern = left_pattern.T
    packed_right = pack(pack_right_kernel, "pack_right", right_pattern, right_values, SLOTS)
    near = [packed_right] + [moved(packed_right, "x", -shift) for shift in SHIFTS[1:]]
    far = [moved(packed_right, "z", -shift) for shift in FAR]
    packed_left = pack(pack_left_kernel, "pack_left", left_pattern, left_values, LEFT_SLOTS)
    own = jnp.concatenate(near, 0)
    packed_left, own = lax.optimization_barrier((packed_left, own))
    up, down = moved(own, "z", 1), moved(own, "z", -1)
    columns = [packed_left] + [moved(packed_left, "y", -shift) for shift in SHIFTS[1:]]
    columns, far, up, down = lax.optimization_barrier((columns, far, up, down))
    far = jnp.concatenate(far, 0)
    far_3, far_1 = moved(far, "x", 1), moved(far, "x", -1)
    mine = jnp.stack(columns)
    left = (mine, moved(mine, "core", 1))
    further_up, further_down = moved(up, "z", 1), moved(down, "z", -1)
    left, far_3, far_1 = lax.optimization_barrier((left, far_3, far_1))
    half = far.shape[0] // 2
    far_2 = (moved(far_3[:half], "x", 1), moved(far_1[half:], "x", -1))
    whole = own.shape[0]
    blocks, copies = [], []
    for piece, z_shift in enumerate((0, -1, 1)):
        blocks += [(z_shift, x_shift) for x_shift in SHIFTS]
        copies.append((piece, 0, whole, piece * whole))
    for n, x_shift in enumerate((0, 3, 1)):
        copies.append((3 + n, 0, 2 * half, len(blocks) * BLOCK))
        blocks += [(z_shift, x_shift) for z_shift in FAR]
    pieces = [own, up, down, far, far_3, far_1]
    (total,) = product(blocks, copies, right_pattern, left_pattern, left, pieces, None, False)
    blocks = [(z_shift, x_shift) for z_shift in (-2, 2) for x_shift in SHIFTS]
    blocks += [(z_shift, 2) for z_shift in FAR]
    copies = [(0, 0, whole, 0), (1, 0, whole, whole), (2, 0, half, 2 * whole), (3, 0, half, 2 * whole + half)]
    pieces = [further_up, further_down, *far_2]
    total, sums = product(blocks, copies, right_pattern, left_pattern, left, pieces, total, True)
    count = lax.axis_size("z") * lax.axis_size("x")
    spread = lax.all_to_all(
        jnp.broadcast_to(sums, (count, sums.shape[1])), COL, 0, 0, tiled=True
    )
    column_mean = jnp.sum(spread, axis=0) / (total.shape[0] * count)
    return total / column_mean[None, :]


def solution(mesh):
    finer = Mesh(mesh.devices.reshape(4, 2, 8, 4), (*ROW, *COL))
    return jax.shard_map(
        shards,
        mesh=finer,
        in_specs=(P(COL, ROW), P(), P(COL, ROW), P()),
        out_specs=P(COL, ROW),
        check_vma=False,
    )
```

```python
import functools

import jax
import jax.numpy as jnp
from jax import lax
from jax.experimental import pallas as pl
from jax.experimental.pallas import tpu as pltpu
from jax.sharding import Mesh
from jax.sharding import PartitionSpec as P

BLOCK = 128
SLOTS = 4
LEFT_SLOTS = 2
SHIFTS = (0, 3, 1, 2)
PLACES = (0, 2, 3, 1)
FAR = (-3, 3, 4)
KERNEL_VMEM = 24 * 1024 * 1024
ROW, COL = ("y", "core"), ("z", "x")


def lanes(start, blocks=1):
    return pl.ds(pl.multiple_of(start * BLOCK, BLOCK), blocks * BLOCK)


def place_of(shift):
    place = jnp.int32(PLACES[3])
    for s in range(3):
        place = jnp.where(shift == s, PLACES[s], place)
    return place


def row_index():
    return lax.axis_index("y") * lax.axis_size("core") + lax.axis_index("core")


def col_index():
    return lax.axis_index("z") * lax.axis_size("x") + lax.axis_index("x")


def pack_right_kernel(pattern, right, out):
    row, col = row_index(), col_index()
    col_blocks = right.shape[1] // BLOCK
    out[...] = jnp.zeros_like(out)
    slot = jnp.int32(0)
    for j in range(col_blocks):
        present = pattern[col, row * col_blocks + j]

        @pl.when(present != 0)
        def _(j=j, slot=slot):
            out[:, lanes(slot)] = right[:, j * BLOCK : (j + 1) * BLOCK]

        slot = slot + present


def pack_left_kernel(pattern, left, out):
    row, col = row_index(), col_index()
    block_rows, inner_blocks = left.shape[0] // BLOCK, left.shape[1] // BLOCK
    out[...] = jnp.zeros_like(out)
    for i in range(block_rows):
        rows = slice(i * BLOCK, (i + 1) * BLOCK)
        slot = jnp.int32(0)
        for k in range(inner_blocks):
            present = pattern[row * inner_blocks + k, col * block_rows + i]

            @pl.when(present != 0)
            def _(k=k, slot=slot, rows=rows):
                out[rows, lanes(slot)] = left[rows, k * BLOCK : (k + 1) * BLOCK]

            slot = slot + present


def pack(kernel, name, pattern, values, slots):
    return pl.pallas_call(
        kernel,
        out_shape=jax.ShapeDtypeStruct((values.shape[0], slots * BLOCK), values.dtype),
        in_specs=[
            pl.BlockSpec(memory_space=pltpu.SMEM),
            pl.BlockSpec(memory_space=pltpu.VMEM),
        ],
        out_specs=pl.BlockSpec(memory_space=pltpu.VMEM),
        compiler_params=pltpu.CompilerParams(vmem_limit_bytes=4 * 1024 * 1024),
        name=name,
    )(pattern, values)


def product_kernel(blocks, copies, first, last, *refs):
    refs = list(refs)
    right_hbm, left_hbm, mine, other = [refs.pop(0) for _ in range(4)]
    pieces = [refs.pop(0) for _ in range(1 + max(copy[0] for copy in copies))]
    total = None if first else refs.pop(0)
    out = refs.pop(0)
    sums = refs.pop(0) if last else None
    right_pattern, left_pattern, plan, *refs = refs
    packed_left, packed_right, dense_left, dense_right, sem, pattern_sem = refs
    row, col = row_index(), col_index()
    y, core = lax.axis_index("y"), lax.axis_index("core")
    z, x = lax.axis_index("z"), lax.axis_index("x")
    y_size, z_size, x_size = lax.axis_size("y"), lax.axis_size("z"), lax.axis_size("x")
    cores = lax.axis_size("core")
    block_rows = dense_left.shape[0] // BLOCK
    col_blocks = dense_right.shape[1] // BLOCK
    z_shifts = sorted({block[0] for block in blocks})
    groups = [lax.rem(z + shift + z_size, z_size) for shift in z_shifts]
    patterns = [
        pltpu.make_async_copy(right_hbm, right_pattern, pattern_sem.at[0]),
        pltpu.make_async_copy(left_hbm, left_pattern, pattern_sem.at[1]),
    ]
    for copy in patterns:
        copy.start()
    waits = []
    for n, group in enumerate(groups):
        there = place_of(lax.rem(lax.div(group, cores) - y + y_size, y_size))
        same = lax.rem(group, cores) == core
        for source, wanted in ((mine, same), (other, jnp.logical_not(same))):
            copy = pltpu.make_async_copy(
                source.at[there], packed_left.at[n, :, : LEFT_SLOTS * BLOCK], sem.at[n]
            )
            pl.when(wanted)(copy.start)
        waits.append(copy)
    for c, (piece, start, rows, to) in enumerate(copies):
        copy = pltpu.make_async_copy(
            pieces[piece].at[pl.ds(start, rows)],
            packed_right.at[pl.ds(to, rows), : SLOTS * BLOCK],
            sem.at[len(groups) + c],
        )
        copy.start()
        waits.append(copy)
    packed_left[:, :, LEFT_SLOTS * BLOCK :] = jnp.zeros(
        (len(groups), packed_left.shape[1], BLOCK), packed_left.dtype
    )
    packed_right[:, SLOTS * BLOCK :] = jnp.zeros(
        (packed_right.shape[0], BLOCK), packed_right.dtype
    )
    for copy in patterns:
        copy.wait()
    for n, group in enumerate(groups):
        for i in range(block_rows):
            slot = jnp.int32(0)
            for inside in range(x_size):
                present = left_pattern[group * x_size + inside, col * block_rows + i]
                source = jnp.where(present != 0, jnp.minimum(slot, LEFT_SLOTS), LEFT_SLOTS)
                plan[(n * block_rows + i) * x_size + inside] = source
                slot = slot + present
    right_plan, left_plan = [], []
    for b, (z_shift, x_shift) in enumerate(blocks):
        n = z_shifts.index(z_shift)
        inside = lax.rem(x + x_shift, x_size)
        k = groups[n] * x_size + inside
        slot = jnp.int32(0)
        for j in range(col_blocks):
            present = right_pattern[k, row * col_blocks + j]
            right_plan.append((b, j, jnp.where(present != 0, jnp.minimum(slot, SLOTS), SLOTS)))
            slot = slot + present
        for i in range(block_rows):
            left_plan.append((n, b, i, plan[(n * block_rows + i) * x_size + inside]))
    for copy in waits:
        copy.wait()
    for b, j, source in right_plan:
        rows = slice(b * BLOCK, (b + 1) * BLOCK)
        dense_right[rows, j * BLOCK : (j + 1) * BLOCK] = packed_right[rows, lanes(source)]
    for n, b, i, source in left_plan:
        rows = slice(i * BLOCK, (i + 1) * BLOCK)
        dense_left[rows, b * BLOCK : (b + 1) * BLOCK] = packed_left[n, rows, lanes(source)]

    width = 256 if last else out.shape[1]

    @pl.loop(0, out.shape[1] // width)
    def _(t):
        columns = pl.ds(pl.multiple_of(t * width, width), width)
        value = jnp.dot(
            dense_left[...], dense_right[:, columns], preferred_element_type=jnp.float32
        )
        if not first:
            value = value + total[:, columns]
        if last:
            value = value * value
            sums[:, columns] = jnp.sum(value, axis=0, keepdims=True)
        out[:, columns] = value


def product(blocks, copies, right_pattern, left_pattern, left, pieces, total, last):
    rows, cols = left[0].shape[1], right_pattern.shape[1] // 8 * BLOCK
    inner = len(blocks) * BLOCK
    groups = len({block[0] for block in blocks})
    out_shape = [jax.ShapeDtypeStruct((rows, cols), jnp.float32)]
    if last:
        out_shape.append(jax.ShapeDtypeStruct((1, cols), jnp.float32))
    vmem = pl.BlockSpec(memory_space=pltpu.VMEM)
    left = [pltpu.with_memory_space_constraint(value, pltpu.HBM) for value in left]
    if not last:
        pieces = [pltpu.with_memory_space_constraint(piece, pltpu.HBM) for piece in pieces]
    operands = [right_pattern, left_pattern, *left, *pieces]
    in_specs = [pl.BlockSpec(memory_space=pl.ANY)] * len(operands)
    aliases = {}
    if total is not None:
        aliases = {len(operands): 0}
        operands.append(total)
        in_specs.append(vmem)
    return pl.pallas_call(
        functools.partial(product_kernel, blocks, copies, total is None, last),
        out_shape=out_shape,
        in_specs=in_specs,
        out_specs=[vmem] * len(out_shape),
        scratch_shapes=[
            pltpu.SMEM(right_pattern.shape, jnp.int32),
            pltpu.SMEM(left_pattern.shape, jnp.int32),
            pltpu.SMEM((groups * rows // BLOCK * 4,), jnp.int32),
            pltpu.VMEM((groups, rows, (LEFT_SLOTS + 1) * BLOCK), jnp.bfloat16),
            pltpu.VMEM((inner, (SLOTS + 1) * BLOCK), jnp.bfloat16),
            pltpu.VMEM((rows, inner), jnp.bfloat16),
            pltpu.VMEM((inner, cols), jnp.bfloat16),
            pltpu.SemaphoreType.DMA((groups + len(copies),)),
            pltpu.SemaphoreType.DMA((2,)),
        ],
        input_output_aliases=aliases,
        compiler_params=pltpu.CompilerParams(vmem_limit_bytes=KERNEL_VMEM),
        cost_estimate=pl.CostEstimate(
            flops=2 * rows * inner * cols, bytes_accessed=4 * 1024 * 1024, transcendentals=0
        ),
        name="product_last" if last else "product_first",
    )(*operands)


def moved(value, axis, step):
    size = lax.axis_size(axis)
    return lax.ppermute(value, axis, [(i, (i + step) % size) for i in range(size)])


def shards(left_values, left_pattern, right_values, right_pattern):
    left_pattern = left_pattern.T
    packed_right = pack(pack_right_kernel, "pack_right", right_pattern, right_values, SLOTS)
    far = [moved(packed_right, "z", -shift) for shift in FAR[:2]]
    near = [packed_right] + [moved(packed_right, "x", -shift) for shift in SHIFTS[1:]]
    packed_left = pack(pack_left_kernel, "pack_left", left_pattern, left_values, LEFT_SLOTS)
    near, packed_left = lax.optimization_barrier((near, packed_left))
    far.append(moved(near[0], "z", -FAR[2]))
    columns = [packed_left] + [moved(packed_left, "y", -shift) for shift in SHIFTS[1:]]
    near, far, columns = lax.optimization_barrier((near, far, columns))
    own, far, mine = jnp.concatenate(near, 0), jnp.concatenate(far, 0), jnp.stack(columns)
    up, down = moved(own, "z", 1), moved(own, "z", -1)
    far_3, far_1 = moved(far, "x", 1), moved(far, "x", -1)
    left = (mine, moved(mine, "core", 1))
    left, up, down, far_3, far_1 = lax.optimization_barrier((left, up, down, far_3, far_1))
    further_up, further_down = moved(up, "z", 1), moved(down, "z", -1)
    half = far.shape[0] // 2
    far_2 = (moved(far_3[:half], "x", 1), moved(far_1[half:], "x", -1))
    whole = own.shape[0]
    blocks, copies = [], []
    for piece, z_shift in enumerate((0, -1, 1)):
        blocks += [(z_shift, x_shift) for x_shift in SHIFTS]
        copies.append((piece, 0, whole, piece * whole))
    for n, x_shift in enumerate((0, 3, 1)):
        copies.append((3 + n, 0, 2 * half, len(blocks) * BLOCK))
        blocks += [(z_shift, x_shift) for z_shift in FAR]
    pieces = [own, up, down, far, far_3, far_1]
    (total,) = product(blocks, copies, right_pattern, left_pattern, left, pieces, None, False)
    blocks = [(z_shift, x_shift) for z_shift in (-2, 2) for x_shift in SHIFTS]
    blocks += [(z_shift, 2) for z_shift in FAR]
    copies = [(0, 0, whole, 0), (1, 0, whole, whole), (2, 0, half, 2 * whole), (3, 0, half, 2 * whole + half)]
    pieces = [further_up, further_down, *far_2]
    total, sums = product(blocks, copies, right_pattern, left_pattern, left, pieces, total, True)
    count = lax.axis_size("z") * lax.axis_size("x")
    spread = lax.all_to_all(
        jnp.broadcast_to(sums, (count, sums.shape[1])), COL, 0, 0, tiled=True
    )
    column_mean = jnp.sum(spread, axis=0) / (total.shape[0] * count)
    return total / column_mean[None, :]


def solution(mesh):
    finer = Mesh(mesh.devices.reshape(4, 2, 8, 4), (*ROW, *COL))
    return jax.shard_map(
        shards,
        mesh=finer,
        in_specs=(P(COL, ROW), P(), P(COL, ROW), P()),
        out_specs=P(COL, ROW),
        check_vma=False,
    )
```

```python
import functools

import jax
import jax.numpy as jnp
from jax import lax
from jax.experimental import pallas as pl
from jax.experimental.pallas import tpu as pltpu
from jax.sharding import Mesh
from jax.sharding import PartitionSpec as P

BLOCK = 128
SLOTS = 4
LEFT_SLOTS = 2
SHIFTS = (0, 3, 1, 2)
KERNEL_VMEM = 24 * 1024 * 1024
ROW, COL = ("y", "core"), ("z", "x")


def lanes(start, blocks=1):
    return pl.ds(pl.multiple_of(start * BLOCK, BLOCK), blocks * BLOCK)


def row_index():
    return lax.axis_index("y") * lax.axis_size("core") + lax.axis_index("core")


def col_index():
    return lax.axis_index("z") * lax.axis_size("x") + lax.axis_index("x")


def pack_right_kernel(pattern, right, out):
    row, col = row_index(), col_index()
    col_blocks = right.shape[1] // BLOCK
    out[...] = jnp.zeros_like(out)
    slot = jnp.int32(0)
    for j in range(col_blocks):
        present = pattern[col, row * col_blocks + j]

        @pl.when(present != 0)
        def _(j=j, slot=slot):
            out[:, lanes(slot)] = right[:, j * BLOCK : (j + 1) * BLOCK]

        slot = slot + present


def pack_left_kernel(pattern, left, out):
    row, col = row_index(), col_index()
    block_rows, inner_blocks = left.shape[0] // BLOCK, left.shape[1] // BLOCK
    out[...] = jnp.zeros_like(out)
    for i in range(block_rows):
        rows = slice(i * BLOCK, (i + 1) * BLOCK)
        slot = jnp.int32(0)
        for k in range(inner_blocks):
            present = pattern[row * inner_blocks + k, col * block_rows + i]

            @pl.when(present != 0)
            def _(k=k, slot=slot, rows=rows):
                out[rows, lanes(slot)] = left[rows, k * BLOCK : (k + 1) * BLOCK]

            slot = slot + present


def pack(kernel, name, pattern, values, slots):
    return pl.pallas_call(
        kernel,
        out_shape=jax.ShapeDtypeStruct((values.shape[0], slots * BLOCK), values.dtype),
        in_specs=[
            pl.BlockSpec(memory_space=pltpu.SMEM),
            pl.BlockSpec(memory_space=pltpu.VMEM),
        ],
        out_specs=pl.BlockSpec(memory_space=pltpu.VMEM),
        compiler_params=pltpu.CompilerParams(vmem_limit_bytes=4 * 1024 * 1024),
        name=name,
    )(pattern, values)


def product_kernel(blocks, copies, first, last, *refs):
    refs = list(refs)
    right_hbm, left_hbm, near_left, sent_left, swapped_left, far_left = [
        refs.pop(0) for _ in range(6)
    ]
    pieces = [refs.pop(0) for _ in range(1 + max(copy[0] for copy in copies))]
    total = None if first else refs.pop(0)
    out = refs.pop(0)
    sums = refs.pop(0) if last else None
    right_pattern, left_pattern, plan, *refs = refs
    packed_left, packed_right, dense_left, dense_right, sem, pattern_sem = refs
    row, col = row_index(), col_index()
    y, core = lax.axis_index("y"), lax.axis_index("core")
    z, x = lax.axis_index("z"), lax.axis_index("x")
    y_size, z_size, x_size = lax.axis_size("y"), lax.axis_size("z"), lax.axis_size("x")
    cores = lax.axis_size("core")
    block_rows = dense_left.shape[0] // BLOCK
    col_blocks = dense_right.shape[1] // BLOCK
    z_shifts = sorted({block[0] for block in blocks})
    groups = [lax.rem(z + shift + z_size, z_size) for shift in z_shifts]
    patterns = [
        pltpu.make_async_copy(right_hbm, right_pattern, pattern_sem.at[0]),
        pltpu.make_async_copy(left_hbm, left_pattern, pattern_sem.at[1]),
    ]
    for copy in patterns:
        copy.start()
    waits = []
    for n, group in enumerate(groups):
        away = lax.rem(lax.div(group, cores) - y + y_size, y_size)
        part = jnp.where(lax.rem(group, cores) == core, 0, 1)
        came = away == jnp.where(core == 0, y_size - 1, 1)
        beside = away == jnp.where(core == 0, 1, y_size - 1)
        for source, index, wanted in (
            (near_left, part, away == 0),
            (sent_left, part, came),
            (swapped_left, 1 - part, beside),
            (far_left, part, away == 2),
        ):
            copy = pltpu.make_async_copy(
                source.at[index], packed_left.at[n, :, : LEFT_SLOTS * BLOCK], sem.at[n]
            )
            pl.when(wanted)(copy.start)
        waits.append(copy)
    for c, (piece, start, rows, to) in enumerate(copies):
        copy = pltpu.make_async_copy(
            pieces[piece].at[pl.ds(start, rows)],
            packed_right.at[pl.ds(to, rows), : SLOTS * BLOCK],
            sem.at[len(groups) + c],
        )
        copy.start()
        waits.append(copy)
    packed_left[:, :, LEFT_SLOTS * BLOCK :] = jnp.zeros(
        (len(groups), packed_left.shape[1], BLOCK), packed_left.dtype
    )
    packed_right[:, SLOTS * BLOCK :] = jnp.zeros(
        (packed_right.shape[0], BLOCK), packed_right.dtype
    )
    for copy in patterns:
        copy.wait()
    for n, group in enumerate(groups):
        for i in range(block_rows):
            slot = jnp.int32(0)
            for inside in range(x_size):
                present = left_pattern[group * x_size + inside, col * block_rows + i]
                source = jnp.where(present != 0, jnp.minimum(slot, LEFT_SLOTS), LEFT_SLOTS)
                plan[(n * block_rows + i) * x_size + inside] = source
                slot = slot + present
    right_plan, left_plan = [], []
    for b, (z_shift, x_shift) in enumerate(blocks):
        n = z_shifts.index(z_shift)
        inside = lax.rem(x + x_shift, x_size)
        k = groups[n] * x_size + inside
        slot = jnp.int32(0)
        for j in range(col_blocks):
            present = right_pattern[k, row * col_blocks + j]
            right_plan.append((b, j, jnp.where(present != 0, jnp.minimum(slot, SLOTS), SLOTS)))
            slot = slot + present
        for i in range(block_rows):
            left_plan.append((n, b, i, plan[(n * block_rows + i) * x_size + inside]))
    for copy in waits:
        copy.wait()
    for b, j, source in right_plan:
        rows = slice(b * BLOCK, (b + 1) * BLOCK)
        dense_right[rows, j * BLOCK : (j + 1) * BLOCK] = packed_right[rows, lanes(source)]
    for n, b, i, source in left_plan:
        rows = slice(i * BLOCK, (i + 1) * BLOCK)
        dense_left[rows, b * BLOCK : (b + 1) * BLOCK] = packed_left[n, rows, lanes(source)]

    width = 256 if last else out.shape[1]

    @pl.loop(0, out.shape[1] // width)
    def _(t):
        columns = pl.ds(pl.multiple_of(t * width, width), width)
        value = jnp.dot(
            dense_left[...], dense_right[:, columns], preferred_element_type=jnp.float32
        )
        if not first:
            value = value + total[:, columns]
        if last:
            value = value * value
            sums[:, columns] = jnp.sum(value, axis=0, keepdims=True)
        out[:, columns] = value


def product(blocks, copies, right_pattern, left_pattern, left, pieces, total, last):
    rows, cols = left[0].shape[1], right_pattern.shape[1] // 8 * BLOCK
    inner = len(blocks) * BLOCK
    groups = len({block[0] for block in blocks})
    out_shape = [jax.ShapeDtypeStruct((rows, cols), jnp.float32)]
    if last:
        out_shape.append(jax.ShapeDtypeStruct((1, cols), jnp.float32))
    vmem = pl.BlockSpec(memory_space=pltpu.VMEM)
    left = [pltpu.with_memory_space_constraint(value, pltpu.HBM) for value in left]
    if not last:
        pieces = [pltpu.with_memory_space_constraint(piece, pltpu.HBM) for piece in pieces]
    operands = [right_pattern, left_pattern, *left, *pieces]
    in_specs = [pl.BlockSpec(memory_space=pl.ANY)] * len(operands)
    aliases = {}
    if total is not None:
        aliases = {len(operands): 0}
        operands.append(total)
        in_specs.append(vmem)
    return pl.pallas_call(
        functools.partial(product_kernel, blocks, copies, total is None, last),
        out_shape=out_shape,
        in_specs=in_specs,
        out_specs=[vmem] * len(out_shape),
        scratch_shapes=[
            pltpu.SMEM(right_pattern.shape, jnp.int32),
            pltpu.SMEM(left_pattern.shape, jnp.int32),
            pltpu.SMEM((groups * rows // BLOCK * 4,), jnp.int32),
            pltpu.VMEM((groups, rows, (LEFT_SLOTS + 1) * BLOCK), jnp.bfloat16),
            pltpu.VMEM((inner, (SLOTS + 1) * BLOCK), jnp.bfloat16),
            pltpu.VMEM((rows, inner), jnp.bfloat16),
            pltpu.VMEM((inner, cols), jnp.bfloat16),
            pltpu.SemaphoreType.DMA((groups + len(copies),)),
            pltpu.SemaphoreType.DMA((2,)),
        ],
        input_output_aliases=aliases,
        compiler_params=pltpu.CompilerParams(vmem_limit_bytes=KERNEL_VMEM),
        cost_estimate=pl.CostEstimate(
            flops=2 * rows * inner * cols, bytes_accessed=4 * 1024 * 1024, transcendentals=0
        ),
        name="product_last" if last else "product_first" if total is None else "product_next",
    )(*operands)


def moved(value, axis, step):
    size = lax.axis_size(axis)
    return lax.ppermute(value, axis, [(i, (i + step) % size) for i in range(size)])


def around(value):
    size, cores = lax.axis_size("y"), lax.axis_size("core")
    pairs = []
    for y in range(size):
        for core in range(cores):
            to = (y + 1) % size if core == 0 else (y - 1) % size
            pairs.append((y * cores + core, to * cores + core))
    return lax.ppermute(value, ("y", "core"), pairs)


def shards(left_values, left_pattern, right_values, right_pattern):
    left_pattern = left_pattern.T
    packed_right = pack(pack_right_kernel, "pack_right", right_pattern, right_values, SLOTS)
    near = [packed_right] + [moved(packed_right, "x", -shift) for shift in SHIFTS[1:]]
    left_values, _ = lax.optimization_barrier((left_values, packed_right))
    packed_left = pack(pack_left_kernel, "pack_left", left_pattern, left_values, LEFT_SLOTS)
    other_left = moved(packed_left, "core", 1)
    near, packed_left, other_left = lax.optimization_barrier((near, packed_left, other_left))
    own = [jnp.concatenate(near[:2], 0), jnp.concatenate(near[2:], 0)]
    half = own[0].shape[0]
    came = {0: own}

    def ring(step):
        came[-step] = [moved(piece, "z", 1) for piece in came[1 - step]]
        came[step] = [moved(piece, "z", -1) for piece in came[step - 1]]

    def tied(values, step):
        values, came[-step][0] = lax.optimization_barrier((values, came[-step][0]))
        return values

    def add(shifts, total, last=False):
        blocks = [(shift, x_shift) for shift in shifts for x_shift in SHIFTS]
        pieces = [piece for shift in shifts for piece in came[shift]]
        copies = [(n, 0, half, n * half) for n in range(len(pieces))]
        return product(blocks, copies, right_pattern, left_pattern, left, pieces, total, last)

    ring(1)
    near_left = jnp.stack([packed_left, other_left])
    sent_left = tied(around(near_left), 1)
    ring(2)
    left = tied([near_left, sent_left, moved(sent_left, "core", 1), around(sent_left)], 2)
    ring(3)
    total = tied(add((0, -1, 1), None)[0], 3)
    came[4] = [moved(came[-3][0], "z", 1), moved(came[3][1], "z", -1)]
    (total,) = add((-2, 2, -3, 3), total)
    total, sums = add((4,), total, True)
    count = lax.axis_size("z") * lax.axis_size("x")
    spread = lax.all_to_all(
        jnp.broadcast_to(sums, (count, sums.shape[1])), COL, 0, 0, tiled=True
    )
    return total * ((total.shape[0] * count) / jnp.sum(spread, axis=0))[None, :]


def solution(mesh):
    finer = Mesh(mesh.devices.reshape(4, 2, 8, 4), (*ROW, *COL))
    return jax.shard_map(
        shards,
        mesh=finer,
        in_specs=(P(COL, ROW), P(), P(COL, ROW), P()),
        out_specs=P(COL, ROW),
        check_vma=False,
    )
```

```python
import functools

import jax
import jax.numpy as jnp
from jax import lax
from jax.experimental import pallas as pl
from jax.experimental.pallas import tpu as pltpu
from jax.sharding import Mesh
from jax.sharding import PartitionSpec as P

BLOCK = 128
SLOTS = 4
LEFT_SLOTS = 2
SHIFTS = (0, 3, 1, 2)
FAR = (-3, 3, 4)
KERNEL_VMEM = 24 * 1024 * 1024
ROW, COL = ("y", "core"), ("z", "x")


def lanes(start, blocks=1):
    return pl.ds(pl.multiple_of(start * BLOCK, BLOCK), blocks * BLOCK)


def row_index():
    return lax.axis_index("y") * lax.axis_size("core") + lax.axis_index("core")


def col_index():
    return lax.axis_index("z") * lax.axis_size("x") + lax.axis_index("x")


def pack_right_kernel(pattern, right, out):
    row, col = row_index(), col_index()
    col_blocks = right.shape[1] // BLOCK
    out[...] = jnp.zeros_like(out)
    slot = jnp.int32(0)
    for j in range(col_blocks):
        present = pattern[col, row * col_blocks + j]

        @pl.when(present != 0)
        def _(j=j, slot=slot):
            out[:, lanes(slot)] = right[:, j * BLOCK : (j + 1) * BLOCK]

        slot = slot + present


def pack_left_kernel(pattern, left, out):
    row, col = row_index(), col_index()
    block_rows, inner_blocks = left.shape[0] // BLOCK, left.shape[1] // BLOCK
    out[...] = jnp.zeros_like(out)
    for i in range(block_rows):
        rows = slice(i * BLOCK, (i + 1) * BLOCK)
        slot = jnp.int32(0)
        for k in range(inner_blocks):
            present = pattern[row * inner_blocks + k, col * block_rows + i]

            @pl.when(present != 0)
            def _(k=k, slot=slot, rows=rows):
                out[rows, lanes(slot)] = left[rows, k * BLOCK : (k + 1) * BLOCK]

            slot = slot + present


def pack(kernel, name, pattern, values, slots):
    return pl.pallas_call(
        kernel,
        out_shape=jax.ShapeDtypeStruct((values.shape[0], slots * BLOCK), values.dtype),
        in_specs=[
            pl.BlockSpec(memory_space=pltpu.SMEM),
            pl.BlockSpec(memory_space=pltpu.VMEM),
        ],
        out_specs=pl.BlockSpec(memory_space=pltpu.VMEM),
        compiler_params=pltpu.CompilerParams(vmem_limit_bytes=4 * 1024 * 1024),
        name=name,
    )(pattern, values)


def product_kernel(blocks, copies, first, last, *refs):
    refs = list(refs)
    right_hbm, left_hbm, near_left, sent_left, swapped_left, far_left = [
        refs.pop(0) for _ in range(6)
    ]
    pieces = [refs.pop(0) for _ in range(1 + max(copy[0] for copy in copies))]
    total = None if first else refs.pop(0)
    out = refs.pop(0)
    sums = refs.pop(0) if last else None
    right_pattern, left_pattern, plan, *refs = refs
    packed_left, packed_right, dense_left, dense_right, sem, pattern_sem = refs
    row, col = row_index(), col_index()
    y, core = lax.axis_index("y"), lax.axis_index("core")
    z, x = lax.axis_index("z"), lax.axis_index("x")
    y_size, z_size, x_size = lax.axis_size("y"), lax.axis_size("z"), lax.axis_size("x")
    cores = lax.axis_size("core")
    block_rows = dense_left.shape[0] // BLOCK
    col_blocks = dense_right.shape[1] // BLOCK
    z_shifts = sorted({block[0] for block in blocks})
    groups = [lax.rem(z + shift + z_size, z_size) for shift in z_shifts]
    patterns = [
        pltpu.make_async_copy(right_hbm, right_pattern, pattern_sem.at[0]),
        pltpu.make_async_copy(left_hbm, left_pattern, pattern_sem.at[1]),
    ]
    for copy in patterns:
        copy.start()
    waits = []
    for n, group in enumerate(groups):
        away = lax.rem(lax.div(group, cores) - y + y_size, y_size)
        part = jnp.where(lax.rem(group, cores) == core, 0, 1)
        came = away == jnp.where(core == 0, y_size - 1, 1)
        beside = away == jnp.where(core == 0, 1, y_size - 1)
        for source, index, wanted in (
            (near_left, part, away == 0),
            (sent_left, part, came),
            (swapped_left, 1 - part, beside),
            (far_left, part, away == 2),
        ):
            copy = pltpu.make_async_copy(
                source.at[index], packed_left.at[n, :, : LEFT_SLOTS * BLOCK], sem.at[n]
            )
            pl.when(wanted)(copy.start)
        waits.append(copy)
    for c, (piece, start, rows, to) in enumerate(copies):
        copy = pltpu.make_async_copy(
            pieces[piece].at[pl.ds(start, rows)],
            packed_right.at[pl.ds(to, rows), : SLOTS * BLOCK],
            sem.at[len(groups) + c],
        )
        copy.start()
        waits.append(copy)
    packed_left[:, :, LEFT_SLOTS * BLOCK :] = jnp.zeros(
        (len(groups), packed_left.shape[1], BLOCK), packed_left.dtype
    )
    packed_right[:, SLOTS * BLOCK :] = jnp.zeros(
        (packed_right.shape[0], BLOCK), packed_right.dtype
    )
    for copy in patterns:
        copy.wait()
    for n, group in enumerate(groups):
        for i in range(block_rows):
            slot = jnp.int32(0)
            for inside in range(x_size):
                present = left_pattern[group * x_size + inside, col * block_rows + i]
                source = jnp.where(present != 0, jnp.minimum(slot, LEFT_SLOTS), LEFT_SLOTS)
                plan[(n * block_rows + i) * x_size + inside] = source
                slot = slot + present
    right_plan, left_plan = [], []
    for b, (z_shift, x_shift) in enumerate(blocks):
        n = z_shifts.index(z_shift)
        inside = lax.rem(x + x_shift, x_size)
        k = groups[n] * x_size + inside
        slot = jnp.int32(0)
        for j in range(col_blocks):
            present = right_pattern[k, row * col_blocks + j]
            right_plan.append((b, j, jnp.where(present != 0, jnp.minimum(slot, SLOTS), SLOTS)))
            slot = slot + present
        for i in range(block_rows):
            left_plan.append((n, b, i, plan[(n * block_rows + i) * x_size + inside]))
    for copy in waits:
        copy.wait()
    for b, j, source in right_plan:
        rows = slice(b * BLOCK, (b + 1) * BLOCK)
        dense_right[rows, j * BLOCK : (j + 1) * BLOCK] = packed_right[rows, lanes(source)]
    for n, b, i, source in left_plan:
        rows = slice(i * BLOCK, (i + 1) * BLOCK)
        dense_left[rows, b * BLOCK : (b + 1) * BLOCK] = packed_left[n, rows, lanes(source)]

    width = 256 if last else out.shape[1]

    @pl.loop(0, out.shape[1] // width)
    def _(t):
        columns = pl.ds(pl.multiple_of(t * width, width), width)
        value = jnp.dot(
            dense_left[...], dense_right[:, columns], preferred_element_type=jnp.float32
        )
        if not first:
            value = value + total[:, columns]
        if last:
            value = value * value
            sums[:, columns] = jnp.sum(value, axis=0, keepdims=True)
        out[:, columns] = value


def product(blocks, copies, right_pattern, left_pattern, left, pieces, total, last):
    rows, cols = left[0].shape[1], right_pattern.shape[1] // 8 * BLOCK
    inner = len(blocks) * BLOCK
    groups = len({block[0] for block in blocks})
    out_shape = [jax.ShapeDtypeStruct((rows, cols), jnp.float32)]
    if last:
        out_shape.append(jax.ShapeDtypeStruct((1, cols), jnp.float32))
    vmem = pl.BlockSpec(memory_space=pltpu.VMEM)
    left = [pltpu.with_memory_space_constraint(value, pltpu.HBM) for value in left]
    if not last:
        pieces = [pltpu.with_memory_space_constraint(piece, pltpu.HBM) for piece in pieces]
    operands = [right_pattern, left_pattern, *left, *pieces]
    in_specs = [pl.BlockSpec(memory_space=pl.ANY)] * len(operands)
    aliases = {}
    if total is not None:
        aliases = {len(operands): 0}
        operands.append(total)
        in_specs.append(vmem)
    return pl.pallas_call(
        functools.partial(product_kernel, blocks, copies, total is None, last),
        out_shape=out_shape,
        in_specs=in_specs,
        out_specs=[vmem] * len(out_shape),
        scratch_shapes=[
            pltpu.SMEM(right_pattern.shape, jnp.int32),
            pltpu.SMEM(left_pattern.shape, jnp.int32),
            pltpu.SMEM((groups * rows // BLOCK * 4,), jnp.int32),
            pltpu.VMEM((groups, rows, (LEFT_SLOTS + 1) * BLOCK), jnp.bfloat16),
            pltpu.VMEM((inner, (SLOTS + 1) * BLOCK), jnp.bfloat16),
            pltpu.VMEM((rows, inner), jnp.bfloat16),
            pltpu.VMEM((inner, cols), jnp.bfloat16),
            pltpu.SemaphoreType.DMA((groups + len(copies),)),
            pltpu.SemaphoreType.DMA((2,)),
        ],
        input_output_aliases=aliases,
        compiler_params=pltpu.CompilerParams(vmem_limit_bytes=KERNEL_VMEM),
        cost_estimate=pl.CostEstimate(
            flops=2 * rows * inner * cols, bytes_accessed=4 * 1024 * 1024, transcendentals=0
        ),
        name="product_last" if last else "product_first" if total is None else "product_next",
    )(*operands)


def moved(value, axis, step):
    size = lax.axis_size(axis)
    return lax.ppermute(value, axis, [(i, (i + step) % size) for i in range(size)])


def around(value):
    size, cores = lax.axis_size("y"), lax.axis_size("core")
    pairs = []
    for y in range(size):
        for core in range(cores):
            to = (y + 1) % size if core == 0 else (y - 1) % size
            pairs.append((y * cores + core, to * cores + core))
    return lax.ppermute(value, ("y", "core"), pairs)


def shards(left_values, left_pattern, right_values, right_pattern):
    left_pattern = left_pattern.T
    packed_right = pack(pack_right_kernel, "pack_right", right_pattern, right_values, SLOTS)
    near = [packed_right] + [moved(packed_right, "x", -shift) for shift in SHIFTS[1:]]
    far = [moved(packed_right, "z", -shift) for shift in FAR[:2]]
    left_values, _ = lax.optimization_barrier((left_values, packed_right))
    packed_left = pack(pack_left_kernel, "pack_left", left_pattern, left_values, LEFT_SLOTS)
    other_left = moved(packed_left, "core", 1)
    near, packed_left, other_left = lax.optimization_barrier((near, packed_left, other_left))
    own = jnp.concatenate(near, 0)
    up, down = moved(own, "z", 1), moved(own, "z", -1)
    near_left = jnp.stack([packed_left, other_left])
    sent_left = around(near_left)
    far, sent_left = lax.optimization_barrier((far, sent_left))
    far.append(moved(far[0], "z", 1))
    left = [near_left, sent_left, moved(sent_left, "core", 1), around(sent_left)]
    up, down, far, left = lax.optimization_barrier((up, down, far, left))
    far = jnp.concatenate(far, 0)
    further_up, further_down = moved(up, "z", 1), moved(down, "z", -1)
    far_3, far_1 = moved(far, "x", 1), moved(far, "x", -1)
    whole, half = own.shape[0], far.shape[0] // 2

    def add(blocks, copies, pieces, total, last=False):
        return product(blocks, copies, right_pattern, left_pattern, left, pieces, total, last)

    blocks = [(z_shift, x_shift) for z_shift in (0, -1, 1) for x_shift in SHIFTS]
    blocks += [(z_shift, 0) for z_shift in FAR]
    copies = [(0, 0, whole, 0), (1, 0, whole, whole), (2, 0, whole, 2 * whole)]
    copies += [(3, 0, 2 * half, 3 * whole)]
    (total,) = add(blocks, copies, [own, up, down, far], None)
    total, far_3, far_1 = lax.optimization_barrier((total, far_3, far_1))
    far_2 = (moved(far_3[:half], "x", 1), moved(far_1[half:], "x", -1))
    blocks = [(z_shift, x_shift) for x_shift in (3, 1) for z_shift in FAR]
    copies = [(0, 0, 2 * half, 0), (1, 0, 2 * half, 2 * half)]
    (total,) = add(blocks, copies, [far_3, far_1], total)
    blocks = [(z_shift, x_shift) for z_shift in (-2, 2) for x_shift in SHIFTS]
    blocks += [(z_shift, 2) for z_shift in FAR]
    copies = [(0, 0, whole, 0), (1, 0, whole, whole)]
    copies += [(2, 0, half, 2 * whole), (3, 0, half, 2 * whole + half)]
    total, sums = add(blocks, copies, [further_up, further_down, *far_2], total, True)
    count = lax.axis_size("z") * lax.axis_size("x")
    spread = lax.all_to_all(
        jnp.broadcast_to(sums, (count, sums.shape[1])), COL, 0, 0, tiled=True
    )
    return total * ((total.shape[0] * count) / jnp.sum(spread, axis=0))[None, :]


def solution(mesh):
    finer = Mesh(mesh.devices.reshape(4, 2, 8, 4), (*ROW, *COL))
    return jax.shard_map(
        shards,
        mesh=finer,
        in_specs=(P(COL, ROW), P(), P(COL, ROW), P()),
        out_specs=P(COL, ROW),
        check_vma=False,
    )
```

```python
import functools

import jax
import jax.numpy as jnp
from jax import lax
from jax.experimental import pallas as pl
from jax.experimental.pallas import tpu as pltpu
from jax.sharding import Mesh
from jax.sharding import PartitionSpec as P

BLOCK = 128
SLOTS = 4
LEFT_SLOTS = 2
SHIFTS = (0, 3, 1, 2)
KERNEL_VMEM = 24 * 1024 * 1024
ROW, COL = ("y", "core"), ("z", "x")


def lanes(start, blocks=1):
    return pl.ds(pl.multiple_of(start * BLOCK, BLOCK), blocks * BLOCK)


def row_index():
    return lax.axis_index("y") * lax.axis_size("core") + lax.axis_index("core")


def col_index():
    return lax.axis_index("z") * lax.axis_size("x") + lax.axis_index("x")


def pack_right_kernel(pattern, right, out):
    row, col = row_index(), col_index()
    col_blocks = right.shape[1] // BLOCK
    out[...] = jnp.zeros_like(out)
    slot = jnp.int32(0)
    for j in range(col_blocks):
        present = pattern[col, row * col_blocks + j]

        @pl.when(present != 0)
        def _(j=j, slot=slot):
            out[:, lanes(slot)] = right[:, j * BLOCK : (j + 1) * BLOCK]

        slot = slot + present


def pack_left_kernel(pattern, left, out):
    row, col = row_index(), col_index()
    block_rows, inner_blocks = left.shape[0] // BLOCK, left.shape[1] // BLOCK
    out[...] = jnp.zeros_like(out)
    for i in range(block_rows):
        rows = slice(i * BLOCK, (i + 1) * BLOCK)
        slot = jnp.int32(0)
        for k in range(inner_blocks):
            present = pattern[row * inner_blocks + k, col * block_rows + i]

            @pl.when(present != 0)
            def _(k=k, slot=slot, rows=rows):
                out[rows, lanes(slot)] = left[rows, k * BLOCK : (k + 1) * BLOCK]

            slot = slot + present


def pack(kernel, name, pattern, values, slots):
    return pl.pallas_call(
        kernel,
        out_shape=jax.ShapeDtypeStruct((values.shape[0], slots * BLOCK), values.dtype),
        in_specs=[
            pl.BlockSpec(memory_space=pltpu.SMEM),
            pl.BlockSpec(memory_space=pltpu.VMEM),
        ],
        out_specs=pl.BlockSpec(memory_space=pltpu.VMEM),
        compiler_params=pltpu.CompilerParams(vmem_limit_bytes=4 * 1024 * 1024),
        name=name,
    )(pattern, values)


def product_kernel(blocks, copies, first, last, *refs):
    refs = list(refs)
    right_hbm, left_hbm, near_left, sent_left, swapped_left, far_left = [
        refs.pop(0) for _ in range(6)
    ]
    pieces = [refs.pop(0) for _ in range(1 + max(copy[0] for copy in copies))]
    total = None if first else refs.pop(0)
    out = refs.pop(0)
    sums = refs.pop(0) if last else None
    right_pattern, left_pattern, plan, *refs = refs
    packed_left, packed_right, dense_left, dense_right, sem, pattern_sem = refs
    row, col = row_index(), col_index()
    y, core = lax.axis_index("y"), lax.axis_index("core")
    z, x = lax.axis_index("z"), lax.axis_index("x")
    y_size, z_size, x_size = lax.axis_size("y"), lax.axis_size("z"), lax.axis_size("x")
    cores = lax.axis_size("core")
    block_rows = dense_left.shape[0] // BLOCK
    col_blocks = dense_right.shape[1] // BLOCK
    z_shifts = sorted({block[0] for block in blocks})
    groups = [lax.rem(z + shift + z_size, z_size) for shift in z_shifts]
    patterns = [
        pltpu.make_async_copy(right_hbm, right_pattern, pattern_sem.at[0]),
        pltpu.make_async_copy(left_hbm, left_pattern, pattern_sem.at[1]),
    ]
    for copy in patterns:
        copy.start()
    waits = []
    for n, group in enumerate(groups):
        away = lax.rem(lax.div(group, cores) - y + y_size, y_size)
        part = jnp.where(lax.rem(group, cores) == core, 0, 1)
        came = away == jnp.where(core == 0, y_size - 1, 1)
        beside = away == jnp.where(core == 0, 1, y_size - 1)
        for source, index, wanted in (
            (near_left, part, away == 0),
            (sent_left, part, came),
            (swapped_left, 1 - part, beside),
            (far_left, part, away == 2),
        ):
            copy = pltpu.make_async_copy(
                source.at[index], packed_left.at[n, :, : LEFT_SLOTS * BLOCK], sem.at[n]
            )
            pl.when(wanted)(copy.start)
        waits.append(copy)
    for c, (piece, start, rows, to) in enumerate(copies):
        copy = pltpu.make_async_copy(
            pieces[piece].at[pl.ds(start, rows)],
            packed_right.at[pl.ds(to, rows), : SLOTS * BLOCK],
            sem.at[len(groups) + c],
        )
        copy.start()
        waits.append(copy)
    packed_left[:, :, LEFT_SLOTS * BLOCK :] = jnp.zeros(
        (len(groups), packed_left.shape[1], BLOCK), packed_left.dtype
    )
    packed_right[:, SLOTS * BLOCK :] = jnp.zeros(
        (packed_right.shape[0], BLOCK), packed_right.dtype
    )
    for copy in patterns:
        copy.wait()
    for n, group in enumerate(groups):
        for i in range(block_rows):
            slot = jnp.int32(0)
            for inside in range(x_size):
                present = left_pattern[group * x_size + inside, col * block_rows + i]
                source = jnp.where(present != 0, jnp.minimum(slot, LEFT_SLOTS), LEFT_SLOTS)
                plan[(n * block_rows + i) * x_size + inside] = source
                slot = slot + present
    right_plan, left_plan = [], []
    for b, (z_shift, x_shift) in enumerate(blocks):
        n = z_shifts.index(z_shift)
        inside = lax.rem(x + x_shift, x_size)
        k = groups[n] * x_size + inside
        slot = jnp.int32(0)
        for j in range(col_blocks):
            present = right_pattern[k, row * col_blocks + j]
            right_plan.append((b, j, jnp.where(present != 0, jnp.minimum(slot, SLOTS), SLOTS)))
            slot = slot + present
        for i in range(block_rows):
            left_plan.append((n, b, i, plan[(n * block_rows + i) * x_size + inside]))
    for copy in waits:
        copy.wait()
    for b, j, source in right_plan:
        rows = slice(b * BLOCK, (b + 1) * BLOCK)
        dense_right[rows, j * BLOCK : (j + 1) * BLOCK] = packed_right[rows, lanes(source)]
    for n, b, i, source in left_plan:
        rows = slice(i * BLOCK, (i + 1) * BLOCK)
        dense_left[rows, b * BLOCK : (b + 1) * BLOCK] = packed_left[n, rows, lanes(source)]

    width = 256 if last else out.shape[1]

    @pl.loop(0, out.shape[1] // width)
    def _(t):
        columns = pl.ds(pl.multiple_of(t * width, width), width)
        value = jnp.dot(
            dense_left[...], dense_right[:, columns], preferred_element_type=jnp.float32
        )
        if not first:
            value = value + total[:, columns]
        if last:
            value = value * value
            sums[:, columns] = jnp.sum(value, axis=0, keepdims=True)
        out[:, columns] = value


def product(blocks, copies, right_pattern, left_pattern, left, pieces, total, last):
    rows, cols = left[0].shape[1], right_pattern.shape[1] // 8 * BLOCK
    inner = len(blocks) * BLOCK
    groups = len({block[0] for block in blocks})
    out_shape = [jax.ShapeDtypeStruct((rows, cols), jnp.float32)]
    if last:
        out_shape.append(jax.ShapeDtypeStruct((1, cols), jnp.float32))
    vmem = pl.BlockSpec(memory_space=pltpu.VMEM)
    left = [pltpu.with_memory_space_constraint(value, pltpu.HBM) for value in left]
    if not last:
        pieces = [pltpu.with_memory_space_constraint(piece, pltpu.HBM) for piece in pieces]
    operands = [right_pattern, left_pattern, *left, *pieces]
    in_specs = [pl.BlockSpec(memory_space=pl.ANY)] * len(operands)
    aliases = {}
    if total is not None:
        aliases = {len(operands): 0}
        operands.append(total)
        in_specs.append(vmem)
    return pl.pallas_call(
        functools.partial(product_kernel, blocks, copies, total is None, last),
        out_shape=out_shape,
        in_specs=in_specs,
        out_specs=[vmem] * len(out_shape),
        scratch_shapes=[
            pltpu.SMEM(right_pattern.shape, jnp.int32),
            pltpu.SMEM(left_pattern.shape, jnp.int32),
            pltpu.SMEM((groups * rows // BLOCK * 4,), jnp.int32),
            pltpu.VMEM((groups, rows, (LEFT_SLOTS + 1) * BLOCK), jnp.bfloat16),
            pltpu.VMEM((inner, (SLOTS + 1) * BLOCK), jnp.bfloat16),
            pltpu.VMEM((rows, inner), jnp.bfloat16),
            pltpu.VMEM((inner, cols), jnp.bfloat16),
            pltpu.SemaphoreType.DMA((groups + len(copies),)),
            pltpu.SemaphoreType.DMA((2,)),
        ],
        input_output_aliases=aliases,
        compiler_params=pltpu.CompilerParams(vmem_limit_bytes=KERNEL_VMEM),
        cost_estimate=pl.CostEstimate(
            flops=2 * rows * inner * cols, bytes_accessed=4 * 1024 * 1024, transcendentals=0
        ),
        name="product_last" if last else "product_first" if total is None else "product_next",
    )(*operands)


def moved(value, axis, step):
    size = lax.axis_size(axis)
    return lax.ppermute(value, axis, [(i, (i + step) % size) for i in range(size)])


def around(value):
    size, cores = lax.axis_size("y"), lax.axis_size("core")
    pairs = []
    for y in range(size):
        for core in range(cores):
            to = (y + 1) % size if core == 0 else (y - 1) % size
            pairs.append((y * cores + core, to * cores + core))
    return lax.ppermute(value, ("y", "core"), pairs)


def shards(left_values, left_pattern, right_values, right_pattern):
    left_pattern = left_pattern.T
    packed_right = pack(pack_right_kernel, "pack_right", right_pattern, right_values, SLOTS)
    near = [packed_right] + [moved(packed_right, "x", -shift) for shift in SHIFTS[1:]]
    left_values, _ = lax.optimization_barrier((left_values, packed_right))
    packed_left = pack(pack_left_kernel, "pack_left", left_pattern, left_values, LEFT_SLOTS)
    near, packed_left = lax.optimization_barrier((near, packed_left))
    other_left = moved(packed_left, "core", 1)
    came = {0: jnp.concatenate(near, 0)}
    whole = came[0].shape[0]
    half = whole // 2

    def ring(step):
        came[-step] = moved(came[1 - step], "z", 1)
        came[step] = moved(came[step - 1], "z", -1)

    def add(shifts, total, pieces, last=False):
        blocks = [(shift, x_shift) for shift in shifts for x_shift in SHIFTS]
        rows = pieces[0].shape[0]
        copies = [(n, 0, rows, n * rows) for n in range(len(pieces))]
        return product(blocks, copies, right_pattern, left_pattern, left, pieces, total, last)

    ring(1)
    near_left = jnp.stack([packed_left, other_left])
    sent_left = around(near_left)
    sent_left, came[-1], came[1] = lax.optimization_barrier((sent_left, came[-1], came[1]))
    ring(2)
    left = [near_left, sent_left, moved(sent_left, "core", 1), around(sent_left)]
    left, came[-2], came[2] = lax.optimization_barrier((left, came[-2], came[2]))
    ring(3)
    shifts = (0, -1, 1, -2, 2)
    (total,) = add(shifts, None, [came[shift] for shift in shifts])
    total, came[-3], came[3] = lax.optimization_barrier((total, came[-3], came[3]))
    far = [moved(came[-3][:half], "z", 1), moved(came[3][half:], "z", -1)]
    (total,) = add((-3, 3), total, [came[-3], came[3]])
    total, sums = add((4,), total, far, True)
    count = lax.axis_size("z") * lax.axis_size("x")
    spread = lax.all_to_all(
        jnp.broadcast_to(sums, (count, sums.shape[1])), COL, 0, 0, tiled=True
    )
    return total * ((total.shape[0] * count) / jnp.sum(spread, axis=0))[None, :]


def solution(mesh):
    finer = Mesh(mesh.devices.reshape(4, 2, 8, 4), (*ROW, *COL))
    return jax.shard_map(
        shards,
        mesh=finer,
        in_specs=(P(COL, ROW), P(), P(COL, ROW), P()),
        out_specs=P(COL, ROW),
        check_vma=False,
    )
```

```python
import functools

import jax
import jax.numpy as jnp
from jax import lax
from jax.experimental import pallas as pl
from jax.experimental.pallas import tpu as pltpu
from jax.sharding import Mesh
from jax.sharding import PartitionSpec as P

BLOCK = 128
SLOTS = 4
LEFT_SLOTS = 2
SHIFTS = (0, 3, 1, 2)
KERNEL_VMEM = 24 * 1024 * 1024
ROW, COL = ("y", "core"), ("z", "x")


def lanes(start, blocks=1):
    return pl.ds(pl.multiple_of(start * BLOCK, BLOCK), blocks * BLOCK)


def row_index():
    return lax.axis_index("y") * lax.axis_size("core") + lax.axis_index("core")


def col_index():
    return lax.axis_index("z") * lax.axis_size("x") + lax.axis_index("x")


def pack_right_kernel(pattern_hbm, right_hbm, out, pattern, right, sem):
    copies = [
        pltpu.make_async_copy(pattern_hbm, pattern, sem.at[0]),
        pltpu.make_async_copy(right_hbm, right, sem.at[1]),
    ]
    for copy in copies:
        copy.start()
    row, col = row_index(), col_index()
    col_blocks = right.shape[1] // BLOCK
    out[...] = jnp.zeros_like(out)
    for copy in copies:
        copy.wait()
    slot = jnp.int32(0)
    for j in range(col_blocks):
        present = pattern[col, row * col_blocks + j]

        @pl.when(present != 0)
        def _(j=j, slot=slot):
            out[:, lanes(slot)] = right[:, j * BLOCK : (j + 1) * BLOCK]

        slot = slot + present


def pack_right(pattern, values):
    pattern, values = [
        pltpu.with_memory_space_constraint(value, pltpu.HBM) for value in (pattern, values)
    ]
    return pl.pallas_call(
        pack_right_kernel,
        out_shape=jax.ShapeDtypeStruct((values.shape[0], SLOTS * BLOCK), values.dtype),
        in_specs=[pl.BlockSpec(memory_space=pl.ANY)] * 2,
        out_specs=pl.BlockSpec(memory_space=pltpu.VMEM),
        scratch_shapes=[
            pltpu.SMEM(pattern.shape, pattern.dtype),
            pltpu.VMEM(values.shape, values.dtype),
            pltpu.SemaphoreType.DMA((2,)),
        ],
        compiler_params=pltpu.CompilerParams(vmem_limit_bytes=4 * 1024 * 1024),
        name="pack_right",
    )(pattern, values)


def pack_left_kernel(pattern, left, out):
    row, col = row_index(), col_index()
    block_rows, inner_blocks = left.shape[0] // BLOCK, left.shape[1] // BLOCK
    out[...] = jnp.zeros_like(out)
    for i in range(block_rows):
        rows = slice(i * BLOCK, (i + 1) * BLOCK)
        slot = jnp.int32(0)
        for k in range(inner_blocks):
            present = pattern[row * inner_blocks + k, col * block_rows + i]

            @pl.when(present != 0)
            def _(k=k, slot=slot, rows=rows):
                out[rows, lanes(slot)] = left[rows, k * BLOCK : (k + 1) * BLOCK]

            slot = slot + present


def pack(kernel, name, pattern, values, slots):
    return pl.pallas_call(
        kernel,
        out_shape=jax.ShapeDtypeStruct((values.shape[0], slots * BLOCK), values.dtype),
        in_specs=[
            pl.BlockSpec(memory_space=pltpu.SMEM),
            pl.BlockSpec(memory_space=pltpu.VMEM),
        ],
        out_specs=pl.BlockSpec(memory_space=pltpu.VMEM),
        compiler_params=pltpu.CompilerParams(vmem_limit_bytes=4 * 1024 * 1024),
        name=name,
    )(pattern, values)


def product_kernel(blocks, copies, first, last, *refs):
    refs = list(refs)
    right_hbm, left_hbm, near_left, sent_left, swapped_left, far_left = [
        refs.pop(0) for _ in range(6)
    ]
    pieces = [refs.pop(0) for _ in range(1 + max(copy[0] for copy in copies))]
    total = None if first else refs.pop(0)
    out = refs.pop(0)
    sums = refs.pop(0) if last else None
    right_pattern, left_pattern, plan, *refs = refs
    packed_left, packed_right, dense_left, dense_right, sem, pattern_sem = refs
    row, col = row_index(), col_index()
    y, core = lax.axis_index("y"), lax.axis_index("core")
    z, x = lax.axis_index("z"), lax.axis_index("x")
    y_size, z_size, x_size = lax.axis_size("y"), lax.axis_size("z"), lax.axis_size("x")
    cores = lax.axis_size("core")
    block_rows = dense_left.shape[0] // BLOCK
    col_blocks = dense_right.shape[1] // BLOCK
    z_shifts = sorted({block[0] for block in blocks})
    groups = [lax.rem(z + shift + z_size, z_size) for shift in z_shifts]
    patterns = [
        pltpu.make_async_copy(right_hbm, right_pattern, pattern_sem.at[0]),
        pltpu.make_async_copy(left_hbm, left_pattern, pattern_sem.at[1]),
    ]
    for copy in patterns:
        copy.start()
    waits = []
    for n, group in enumerate(groups):
        away = lax.rem(lax.div(group, cores) - y + y_size, y_size)
        part = jnp.where(lax.rem(group, cores) == core, 0, 1)
        came = away == jnp.where(core == 0, y_size - 1, 1)
        beside = away == jnp.where(core == 0, 1, y_size - 1)
        for source, index, wanted in (
            (near_left, part, away == 0),
            (sent_left, part, came),
            (swapped_left, 1 - part, beside),
            (far_left, part, away == 2),
        ):
            copy = pltpu.make_async_copy(
                source.at[index], packed_left.at[n, :, : LEFT_SLOTS * BLOCK], sem.at[n]
            )
            pl.when(wanted)(copy.start)
        waits.append(copy)
    for c, (piece, start, rows, to) in enumerate(copies):
        copy = pltpu.make_async_copy(
            pieces[piece].at[pl.ds(start, rows)],
            packed_right.at[pl.ds(to, rows), : SLOTS * BLOCK],
            sem.at[len(groups) + c],
        )
        copy.start()
        waits.append(copy)
    packed_left[:, :, LEFT_SLOTS * BLOCK :] = jnp.zeros(
        (len(groups), packed_left.shape[1], BLOCK), packed_left.dtype
    )
    packed_right[:, SLOTS * BLOCK :] = jnp.zeros(
        (packed_right.shape[0], BLOCK), packed_right.dtype
    )
    for copy in patterns:
        copy.wait()
    for n, group in enumerate(groups):
        for i in range(block_rows):
            slot = jnp.int32(0)
            for inside in range(x_size):
                present = left_pattern[group * x_size + inside, col * block_rows + i]
                source = jnp.where(present != 0, jnp.minimum(slot, LEFT_SLOTS), LEFT_SLOTS)
                plan[(n * block_rows + i) * x_size + inside] = source
                slot = slot + present
    right_plan, left_plan = [], []
    for b, (z_shift, x_shift) in enumerate(blocks):
        n = z_shifts.index(z_shift)
        inside = lax.rem(x + x_shift, x_size)
        k = groups[n] * x_size + inside
        slot = jnp.int32(0)
        for j in range(col_blocks):
            present = right_pattern[k, row * col_blocks + j]
            right_plan.append((b, j, jnp.where(present != 0, jnp.minimum(slot, SLOTS), SLOTS)))
            slot = slot + present
        for i in range(block_rows):
            left_plan.append((n, b, i, plan[(n * block_rows + i) * x_size + inside]))
    for copy in waits:
        copy.wait()
    for b, j, source in right_plan:
        rows = slice(b * BLOCK, (b + 1) * BLOCK)
        dense_right[rows, j * BLOCK : (j + 1) * BLOCK] = packed_right[rows, lanes(source)]
    for n, b, i, source in left_plan:
        rows = slice(i * BLOCK, (i + 1) * BLOCK)
        dense_left[rows, b * BLOCK : (b + 1) * BLOCK] = packed_left[n, rows, lanes(source)]

    width = 256 if last else out.shape[1]

    @pl.loop(0, out.shape[1] // width)
    def _(t):
        columns = pl.ds(pl.multiple_of(t * width, width), width)
        value = jnp.dot(
            dense_left[...], dense_right[:, columns], preferred_element_type=jnp.float32
        )
        if not first:
            value = value + total[:, columns]
        if last:
            value = value * value
            sums[:, columns] = jnp.sum(value, axis=0, keepdims=True)
        out[:, columns] = value


def product(blocks, copies, right_pattern, left_pattern, left, pieces, total, last):
    rows, cols = left[0].shape[1], right_pattern.shape[1] // 8 * BLOCK
    inner = len(blocks) * BLOCK
    groups = len({block[0] for block in blocks})
    out_shape = [jax.ShapeDtypeStruct((rows, cols), jnp.float32)]
    if last:
        out_shape.append(jax.ShapeDtypeStruct((1, cols), jnp.float32))
    vmem = pl.BlockSpec(memory_space=pltpu.VMEM)
    left = [pltpu.with_memory_space_constraint(value, pltpu.HBM) for value in left]
    if not last:
        pieces = [pltpu.with_memory_space_constraint(piece, pltpu.HBM) for piece in pieces]
    operands = [right_pattern, left_pattern, *left, *pieces]
    in_specs = [pl.BlockSpec(memory_space=pl.ANY)] * len(operands)
    aliases = {}
    if total is not None:
        aliases = {len(operands): 0}
        operands.append(total)
        in_specs.append(vmem)
    return pl.pallas_call(
        functools.partial(product_kernel, blocks, copies, total is None, last),
        out_shape=out_shape,
        in_specs=in_specs,
        out_specs=[vmem] * len(out_shape),
        scratch_shapes=[
            pltpu.SMEM(right_pattern.shape, jnp.int32),
            pltpu.SMEM(left_pattern.shape, jnp.int32),
            pltpu.SMEM((groups * rows // BLOCK * 4,), jnp.int32),
            pltpu.VMEM((groups, rows, (LEFT_SLOTS + 1) * BLOCK), jnp.bfloat16),
            pltpu.VMEM((inner, (SLOTS + 1) * BLOCK), jnp.bfloat16),
            pltpu.VMEM((rows, inner), jnp.bfloat16),
            pltpu.VMEM((inner, cols), jnp.bfloat16),
            pltpu.SemaphoreType.DMA((groups + len(copies),)),
            pltpu.SemaphoreType.DMA((2,)),
        ],
        input_output_aliases=aliases,
        compiler_params=pltpu.CompilerParams(vmem_limit_bytes=KERNEL_VMEM),
        cost_estimate=pl.CostEstimate(
            flops=2 * rows * inner * cols, bytes_accessed=4 * 1024 * 1024, transcendentals=0
        ),
        name="product_last" if last else "product_first" if total is None else "product_next",
    )(*operands)


def moved(value, axis, step):
    size = lax.axis_size(axis)
    return lax.ppermute(value, axis, [(i, (i + step) % size) for i in range(size)])


def around(value):
    size, cores = lax.axis_size("y"), lax.axis_size("core")
    pairs = []
    for y in range(size):
        for core in range(cores):
            to = (y + 1) % size if core == 0 else (y - 1) % size
            pairs.append((y * cores + core, to * cores + core))
    return lax.ppermute(value, ("y", "core"), pairs)


def shards(left_values, left_pattern, right_values, right_pattern):
    left_pattern = left_pattern.T
    packed_right = pack_right(right_pattern, right_values)
    near = [packed_right] + [moved(packed_right, "x", -shift) for shift in SHIFTS[1:]]
    left_values, _ = lax.optimization_barrier((left_values, packed_right))
    packed_left = pack(pack_left_kernel, "pack_left", left_pattern, left_values, LEFT_SLOTS)
    near, packed_left = lax.optimization_barrier((near, packed_left))
    other_left = moved(packed_left, "core", 1)
    came = {0: jnp.concatenate(near, 0)}
    whole = came[0].shape[0]
    half = whole // 2

    def ring(step):
        came[-step] = moved(came[1 - step], "z", 1)
        came[step] = moved(came[step - 1], "z", -1)

    def add(shifts, total, pieces, last=False):
        blocks = [(shift, x_shift) for shift in shifts for x_shift in SHIFTS]
        rows = pieces[0].shape[0]
        copies = [(n, 0, rows, n * rows) for n in range(len(pieces))]
        return product(blocks, copies, right_pattern, left_pattern, left, pieces, total, last)

    ring(1)
    near_left = jnp.stack([packed_left, other_left])
    sent_left = around(near_left)
    sent_left, came[-1], came[1] = lax.optimization_barrier((sent_left, came[-1], came[1]))
    ring(2)
    left = [near_left, sent_left, moved(sent_left, "core", 1), around(sent_left)]
    left, came[-2], came[2] = lax.optimization_barrier((left, came[-2], came[2]))
    ring(3)
    shifts = (0, -1, 1, -2, 2)
    (total,) = add(shifts, None, [came[shift] for shift in shifts])
    total, came[-3], came[3] = lax.optimization_barrier((total, came[-3], came[3]))
    far = [moved(came[-3][:half], "z", 1), moved(came[3][half:], "z", -1)]
    (total,) = add((-3, 3), total, [came[-3], came[3]])
    total, sums = add((4,), total, far, True)
    count = lax.axis_size("z") * lax.axis_size("x")
    spread = lax.all_to_all(
        jnp.broadcast_to(sums, (count, sums.shape[1])), COL, 0, 0, tiled=True
    )
    return total * ((total.shape[0] * count) / jnp.sum(spread, axis=0))[None, :]


def solution(mesh):
    finer = Mesh(mesh.devices.reshape(4, 2, 8, 4), (*ROW, *COL))
    return jax.shard_map(
        shards,
        mesh=finer,
        in_specs=(P(COL, ROW), P(), P(COL, ROW), P()),
        out_specs=P(COL, ROW),
        check_vma=False,
    )
```

```python
import functools

import jax
import jax.numpy as jnp
from jax import lax
from jax.experimental import pallas as pl
from jax.experimental.pallas import tpu as pltpu
from jax.sharding import Mesh
from jax.sharding import PartitionSpec as P

BLOCK = 128
SLOTS = 4
LEFT_SLOTS = 2
SHIFTS = (0, 3, 1, 2)
KERNEL_VMEM = 24 * 1024 * 1024
ROW, COL = ("y", "core"), ("z", "x")


def lanes(start, blocks=1):
    return pl.ds(pl.multiple_of(start * BLOCK, BLOCK), blocks * BLOCK)


def row_index():
    return lax.axis_index("y") * lax.axis_size("core") + lax.axis_index("core")


def col_index():
    return lax.axis_index("z") * lax.axis_size("x") + lax.axis_index("x")


def pack_right_kernel(pattern_hbm, right_hbm, out, pattern, right, sem):
    copies = [
        pltpu.make_async_copy(pattern_hbm, pattern, sem.at[0]),
        pltpu.make_async_copy(right_hbm, right, sem.at[1]),
    ]
    for copy in copies:
        copy.start()
    row, col = row_index(), col_index()
    col_blocks = right.shape[1] // BLOCK
    out[...] = jnp.zeros_like(out)
    for copy in copies:
        copy.wait()
    slot = jnp.int32(0)
    for j in range(col_blocks):
        present = pattern[col, row * col_blocks + j]

        @pl.when(present != 0)
        def _(j=j, slot=slot):
            out[:, lanes(slot)] = right[:, j * BLOCK : (j + 1) * BLOCK]

        slot = slot + present


def pack_right(pattern, values):
    pattern, values = [
        pltpu.with_memory_space_constraint(value, pltpu.HBM) for value in (pattern, values)
    ]
    return pl.pallas_call(
        pack_right_kernel,
        out_shape=jax.ShapeDtypeStruct((values.shape[0], SLOTS * BLOCK), values.dtype),
        in_specs=[pl.BlockSpec(memory_space=pl.ANY)] * 2,
        out_specs=pl.BlockSpec(memory_space=pltpu.VMEM),
        scratch_shapes=[
            pltpu.SMEM(pattern.shape, pattern.dtype),
            pltpu.VMEM(values.shape, values.dtype),
            pltpu.SemaphoreType.DMA((2,)),
        ],
        compiler_params=pltpu.CompilerParams(vmem_limit_bytes=4 * 1024 * 1024),
        name="pack_right",
    )(pattern, values)


def pack_left_kernel(pattern, left, out):
    row, col = row_index(), col_index()
    block_rows, inner_blocks = left.shape[0] // BLOCK, left.shape[1] // BLOCK
    out[...] = jnp.zeros_like(out)
    for i in range(block_rows):
        rows = slice(i * BLOCK, (i + 1) * BLOCK)
        slot = jnp.int32(0)
        for k in range(inner_blocks):
            present = pattern[row * inner_blocks + k, col * block_rows + i]

            @pl.when(present != 0)
            def _(k=k, slot=slot, rows=rows):
                out[rows, lanes(slot)] = left[rows, k * BLOCK : (k + 1) * BLOCK]

            slot = slot + present


def pack(kernel, name, pattern, values, slots):
    return pl.pallas_call(
        kernel,
        out_shape=jax.ShapeDtypeStruct((values.shape[0], slots * BLOCK), values.dtype),
        in_specs=[
            pl.BlockSpec(memory_space=pltpu.SMEM),
            pl.BlockSpec(memory_space=pltpu.VMEM),
        ],
        out_specs=pl.BlockSpec(memory_space=pltpu.VMEM),
        compiler_params=pltpu.CompilerParams(vmem_limit_bytes=4 * 1024 * 1024),
        name=name,
    )(pattern, values)


def product_kernel(blocks, copies, first, last, *refs):
    refs = list(refs)
    right_hbm, left_hbm, near_left, sent_left, swapped_left, far_left = [
        refs.pop(0) for _ in range(6)
    ]
    pieces = [refs.pop(0) for _ in range(1 + max(copy[0] for copy in copies))]
    total = None if first else refs.pop(0)
    out = refs.pop(0)
    sums = refs.pop(0) if last else None
    right_pattern, left_pattern, plan, *refs = refs
    packed_left, packed_right, dense_left, dense_right, sem, pattern_sem = refs
    row, col = row_index(), col_index()
    y, core = lax.axis_index("y"), lax.axis_index("core")
    z, x = lax.axis_index("z"), lax.axis_index("x")
    y_size, z_size, x_size = lax.axis_size("y"), lax.axis_size("z"), lax.axis_size("x")
    cores = lax.axis_size("core")
    block_rows = dense_left.shape[0] // BLOCK
    col_blocks = dense_right.shape[1] // BLOCK
    z_shifts = sorted({block[0] for block in blocks})
    groups = [lax.rem(z + shift + z_size, z_size) for shift in z_shifts]
    patterns = [
        pltpu.make_async_copy(right_hbm, right_pattern, pattern_sem.at[0]),
        pltpu.make_async_copy(left_hbm, left_pattern, pattern_sem.at[1]),
    ]
    for copy in patterns:
        copy.start()
    waits = []
    for n, group in enumerate(groups):
        away = lax.rem(lax.div(group, cores) - y + y_size, y_size)
        part = jnp.where(lax.rem(group, cores) == core, 0, 1)
        came = away == jnp.where(core == 0, y_size - 1, 1)
        beside = away == jnp.where(core == 0, 1, y_size - 1)
        for source, index, wanted in (
            (near_left, part, away == 0),
            (sent_left, part, came),
            (swapped_left, 1 - part, beside),
            (far_left, part, away == 2),
        ):
            copy = pltpu.make_async_copy(
                source.at[index], packed_left.at[n, :, : LEFT_SLOTS * BLOCK], sem.at[n]
            )
            pl.when(wanted)(copy.start)
        waits.append(copy)
    for c, (piece, start, rows, to) in enumerate(copies):
        copy = pltpu.make_async_copy(
            pieces[piece].at[pl.ds(start, rows)],
            packed_right.at[pl.ds(to, rows), : SLOTS * BLOCK],
            sem.at[len(groups) + c],
        )
        copy.start()
        waits.append(copy)
    packed_left[:, :, LEFT_SLOTS * BLOCK :] = jnp.zeros(
        (len(groups), packed_left.shape[1], BLOCK), packed_left.dtype
    )
    packed_right[:, SLOTS * BLOCK :] = jnp.zeros(
        (packed_right.shape[0], BLOCK), packed_right.dtype
    )
    for copy in patterns:
        copy.wait()
    for n, group in enumerate(groups):
        for i in range(block_rows):
            slot = jnp.int32(0)
            for inside in range(x_size):
                present = left_pattern[group * x_size + inside, col * block_rows + i]
                source = jnp.where(present != 0, jnp.minimum(slot, LEFT_SLOTS), LEFT_SLOTS)
                plan[(n * block_rows + i) * x_size + inside] = source
                slot = slot + present
    right_plan, left_plan = [], []
    for b, (z_shift, x_shift) in enumerate(blocks):
        n = z_shifts.index(z_shift)
        inside = lax.rem(x + x_shift, x_size)
        k = groups[n] * x_size + inside
        slot = jnp.int32(0)
        for j in range(col_blocks):
            present = right_pattern[k, row * col_blocks + j]
            right_plan.append((b, j, jnp.where(present != 0, jnp.minimum(slot, SLOTS), SLOTS)))
            slot = slot + present
        for i in range(block_rows):
            left_plan.append((n, b, i, plan[(n * block_rows + i) * x_size + inside]))
    for copy in waits:
        copy.wait()
    for b, j, source in right_plan:
        rows = slice(b * BLOCK, (b + 1) * BLOCK)
        dense_right[rows, j * BLOCK : (j + 1) * BLOCK] = packed_right[rows, lanes(source)]
    for n, b, i, source in left_plan:
        rows = slice(i * BLOCK, (i + 1) * BLOCK)
        dense_left[rows, b * BLOCK : (b + 1) * BLOCK] = packed_left[n, rows, lanes(source)]

    width = 256 if last else out.shape[1]

    @pl.loop(0, out.shape[1] // width)
    def _(t):
        columns = pl.ds(pl.multiple_of(t * width, width), width)
        value = jnp.dot(
            dense_left[...], dense_right[:, columns], preferred_element_type=jnp.float32
        )
        if not first:
            value = value + total[:, columns]
        if last:
            value = value * value
            sums[:, columns] = jnp.sum(value, axis=0, keepdims=True)
        out[:, columns] = value


def product(blocks, copies, right_pattern, left_pattern, left, pieces, total, last):
    rows, cols = left[0].shape[1], right_pattern.shape[1] // 8 * BLOCK
    inner = len(blocks) * BLOCK
    groups = len({block[0] for block in blocks})
    out_shape = [jax.ShapeDtypeStruct((rows, cols), jnp.float32)]
    if last:
        out_shape.append(jax.ShapeDtypeStruct((1, cols), jnp.float32))
    vmem = pl.BlockSpec(memory_space=pltpu.VMEM)
    left = [pltpu.with_memory_space_constraint(value, pltpu.HBM) for value in left]
    if not last:
        pieces = [pltpu.with_memory_space_constraint(piece, pltpu.HBM) for piece in pieces]
    operands = [right_pattern, left_pattern, *left, *pieces]
    in_specs = [pl.BlockSpec(memory_space=pl.ANY)] * len(operands)
    aliases = {}
    if total is not None:
        aliases = {len(operands): 0}
        operands.append(total)
        in_specs.append(vmem)
    return pl.pallas_call(
        functools.partial(product_kernel, blocks, copies, total is None, last),
        out_shape=out_shape,
        in_specs=in_specs,
        out_specs=[vmem] * len(out_shape),
        scratch_shapes=[
            pltpu.SMEM(right_pattern.shape, jnp.int32),
            pltpu.SMEM(left_pattern.shape, jnp.int32),
            pltpu.SMEM((groups * rows // BLOCK * 4,), jnp.int32),
            pltpu.VMEM((groups, rows, (LEFT_SLOTS + 1) * BLOCK), jnp.bfloat16),
            pltpu.VMEM((inner, (SLOTS + 1) * BLOCK), jnp.bfloat16),
            pltpu.VMEM((rows, inner), jnp.bfloat16),
            pltpu.VMEM((inner, cols), jnp.bfloat16),
            pltpu.SemaphoreType.DMA((groups + len(copies),)),
            pltpu.SemaphoreType.DMA((2,)),
        ],
        input_output_aliases=aliases,
        compiler_params=pltpu.CompilerParams(vmem_limit_bytes=KERNEL_VMEM),
        cost_estimate=pl.CostEstimate(
            flops=2 * rows * inner * cols, bytes_accessed=4 * 1024 * 1024, transcendentals=0
        ),
        name="product_last" if last else "product_first" if total is None else "product_next",
    )(*operands)


def moved(value, axis, step):
    size = lax.axis_size(axis)
    return lax.ppermute(value, axis, [(i, (i + step) % size) for i in range(size)])


def around(value):
    size, cores = lax.axis_size("y"), lax.axis_size("core")
    pairs = []
    for y in range(size):
        for core in range(cores):
            to = (y + 1) % size if core == 0 else (y - 1) % size
            pairs.append((y * cores + core, to * cores + core))
    return lax.ppermute(value, ("y", "core"), pairs)


def shards(left_values, left_pattern, right_values, right_pattern):
    left_pattern = left_pattern.T
    packed_right = pack_right(right_pattern, right_values)
    near = [packed_right] + [moved(packed_right, "x", -shift) for shift in SHIFTS[1:]]
    left_values, _ = lax.optimization_barrier((left_values, packed_right))
    packed_left = pack(pack_left_kernel, "pack_left", left_pattern, left_values, LEFT_SLOTS)
    own, packed_left = lax.optimization_barrier((jnp.concatenate(near, 0), packed_left))
    other_left = moved(packed_left, "core", 1)
    came = {0: own}
    whole = came[0].shape[0]
    half = whole // 2

    def ring(step):
        came[-step] = moved(came[1 - step], "z", 1)
        came[step] = moved(came[step - 1], "z", -1)

    def add(shifts, total, pieces, last=False):
        blocks = [(shift, x_shift) for shift in shifts for x_shift in SHIFTS]
        rows = pieces[0].shape[0]
        copies = [(n, 0, rows, n * rows) for n in range(len(pieces))]
        return product(blocks, copies, right_pattern, left_pattern, left, pieces, total, last)

    ring(1)
    near_left = jnp.stack([packed_left, other_left])
    sent_left = around(near_left)
    sent_left, came[-1], came[1] = lax.optimization_barrier((sent_left, came[-1], came[1]))
    ring(2)
    left = [near_left, sent_left, moved(sent_left, "core", 1), around(sent_left)]
    left, came[-2], came[2] = lax.optimization_barrier((left, came[-2], came[2]))
    ring(3)
    shifts = (0, -1, 1, -2, 2)
    (total,) = add(shifts, None, [came[shift] for shift in shifts])
    total, came[-3], came[3] = lax.optimization_barrier((total, came[-3], came[3]))
    far = [moved(came[-3][:half], "z", 1), moved(came[3][half:], "z", -1)]
    (total,) = add((-3, 3), total, [came[-3], came[3]])
    total, sums = add((4,), total, far, True)
    count = lax.axis_size("z") * lax.axis_size("x")
    spread = lax.all_to_all(
        jnp.broadcast_to(sums, (count, sums.shape[1])), COL, 0, 0, tiled=True
    )
    return total * ((total.shape[0] * count) / jnp.sum(spread, axis=0))[None, :]


def solution(mesh):
    finer = Mesh(mesh.devices.reshape(4, 2, 8, 4), (*ROW, *COL))
    return jax.shard_map(
        shards,
        mesh=finer,
        in_specs=(P(COL, ROW), P(), P(COL, ROW), P()),
        out_specs=P(COL, ROW),
        check_vma=False,
    )
```
